32 devices in a mesh: lvl: 2 (over core), front: 4 (over z), grid: 4 (over y, x).
Axes of the slice: x: 2, y: 2, z: 4, core: 2. Of those that a mesh axis runs over, the one named last changes fastest.
Arguments:
- child_panel: bfloat16 [4, 2, 4, 2, 128, 512], P('front', None, 'grid', 'lvl'), may hold values from -0.6 to 0.6
- child_blocks: int32 [4], P('front'), may hold values from 6 to 8, as said below
- tile_rows: int32 [2, 4, 4, 64], P('lvl', 'front', 'grid'), may hold values from 0 to 1
- tile_cols: int32 [2, 4, 4, 64], P('lvl', 'front', 'grid'), may hold values from 0 to 7
- tile_parent: int32 [2, 4, 4, 64, 1], P('lvl', 'front', 'grid'), may hold values from 0 to 3; in each aligned block of 64 rows (0 to 63, 64 to 127, ..., all dimensions but the last counted through in order) at most 32 rows name the same one
- tile_place: int32 [2, 4, 4, 64], P('lvl', 'front', 'grid'), may hold values from 0 to 15
- parent_owner: int32 [4], replicated, may hold values from 0 to 3, each once
- parent_front: float32 [4, 2, 4, 2, 128, 2048], P('front', None, 'grid', 'lvl'), may hold values from -1.5 to 151.5, as said below
Outputs:
- factored: float32 [4, 2, 4, 2, 128, 2048], P('front', None, 'grid', 'lvl')
The draws below stay inside these ranges and needn't reach their ends.
Inputs may be any that keep to these rules, and one draw needn't show every extreme that they name: `child_blocks`: some child front has exactly 8 blocks. `tile_parent`: among the 64 tiles of one device at most 32 name the same parent front, and some parent front is named by exactly 32. `parent_owner`: each front index holds exactly one parent. `parent_front`: the diagonal of each parent's first diagonal block lies between 148.5 and 151.5; all other entries lie within -1.5 to 1.5.
All inputs are finite; a program needn't handle non-finite values.
Results may differ from the reference program's by a relative error of at most 0.00053.
Values may be sent and summed in bfloat16 or wider, within the bound.
A program may use at most 64 MiB of HBM per device.

```python
import math
import jax
import jax.numpy as jnp
import numpy as np
from jax import lax

BLOCK = 256
PANEL = 512
CHILD_SPAN = 8
PARENT_SPAN = 8
SLOTS_DEV = 64
HALF_ROWS = 128
CHILD_LOCAL = 2
PARENT_LOCAL = 2
CAPACITY = 32
FRONT_WIDTH = 2048
FRONTS = 4
N_LVL = 2
N_GRID = 4


def draw_child_panel(key, part):
    shape = (FRONTS, CHILD_LOCAL, N_GRID, N_LVL, HALF_ROWS, PANEL)
    noise_key = jax.random.fold_in(key, 31)
    values = 0.1 * jnp.clip(jax.random.normal(noise_key, shape, jnp.float32), -6.0, 6.0)
    return values.astype(jnp.bfloat16)


def draw_child_blocks(key, part):
    sizes = jax.random.randint(jax.random.fold_in(key, 11), (FRONTS,), CHILD_SPAN - 2, CHILD_SPAN + 1)
    widest = jax.random.randint(jax.random.fold_in(key, 12), (), 0, FRONTS)
    offset = jax.random.randint(jax.random.fold_in(key, 13), (), 1, FRONTS)
    narrow = (widest + offset) % FRONTS
    places = jnp.arange(FRONTS)
    sizes = jnp.where(places == narrow, CHILD_SPAN - 2, sizes)
    return jnp.where(places == widest, CHILD_SPAN, sizes).astype(jnp.int32)


def draw_parent_front(key, part):
    shape = (FRONTS, PARENT_LOCAL, N_GRID, N_LVL, HALF_ROWS, FRONT_WIDTH)
    noise_key = jax.random.fold_in(key, 21)
    noise = 0.5 * jnp.clip(jax.random.normal(noise_key, shape, jnp.float32), -3.0, 3.0)
    block_row = lax.broadcasted_iota(jnp.int32, shape, 1)
    grid_row = lax.broadcasted_iota(jnp.int32, shape, 2)
    level_row = lax.broadcasted_iota(jnp.int32, shape, 3)
    inner_row = lax.broadcasted_iota(jnp.int32, shape, 4)
    column = lax.broadcasted_iota(jnp.int32, shape, 5)
    diagonal = (block_row == 0) & (grid_row == 0) & (level_row * HALF_ROWS + inner_row == column)
    return (noise + 150.0 * diagonal.astype(jnp.float32)).astype(jnp.float32)


def plant(values, key, low, largest):
    dims = values.shape
    index_at = [jax.random.randint(jax.random.fold_in(key, axis), (), 0, dims[axis]) for axis in range(len(dims))]
    values = values.at[tuple(index_at)].set(low)
    longest = dims.index(max(dims))
    index_at[longest] = (index_at[longest] + 1) % dims[longest]
    return values.at[tuple(index_at)].set(largest)


def assign_block(own_key, own, number, rows, number_of, top, bound, slope):
    sequence = jax.random.permutation(own_key, number_of)
    packed, ordinary = shares(number_of, rows * top, bound, slope, True), shares(number_of, rows * top, bound, slope, False)
    places = jnp.arange(number_of)

    def named(sizes, offset_by):
        used = int((sizes > 0).sum())
        fixed = max(1, used // 4)
        shifted = fixed + (places - fixed + offset_by * (used - fixed)) % max(1, number_of - fixed)
        return jnp.zeros((number_of,), jnp.int32).at[sequence[jnp.where(places < fixed, places, shifted)]].set(jnp.asarray(sizes, jnp.int32))

    sizes = jnp.where(number % 4 == 0, named(packed, number // 4), named(ordinary, number - number // 4 - 1))
    mixed = jax.random.permutation(jax.random.fold_in(own, 3), number_of)
    source_of, sink = mixed[0:number_of // 2 * 2:2], mixed[1:number_of // 2 * 2:2]
    margin = jnp.minimum(sizes[source_of] - 1, bound - sizes[sink]) // 2
    margin = jnp.where((source_of == sequence[0]) | (sink == sequence[0]) | (sizes[sink] == 0), 0, jnp.maximum(margin, 0))
    shifted = jax.random.randint(jax.random.fold_in(own, 4), (number_of // 2,), 0, 1 << 20) % (margin + 1)
    sizes = sizes.at[source_of].add(-shifted).at[sink].add(shifted)
    members = jnp.searchsorted(jnp.cumsum(sizes), jnp.arange(rows * top), side="right").astype(jnp.int32)
    table = members.reshape(top, rows).T
    table = table[jax.random.permutation(jax.random.fold_in(own, 1), rows)]
    offset_by = jax.random.randint(jax.random.fold_in(own, 2), (rows, 1), 0, top)
    return jnp.take_along_axis(table, (jnp.arange(top)[None, :] + offset_by) % top, axis=1)


def shares(count, total, bound, slope, full):
    weights = [(1 << 20) // math.isqrt(rank ** slope) + 1 for rank in range(1, count + 1)]
    largest = bound if full else min(bound, max(-(-total // count), total * weights[0] // sum(weights)))
    least = 1 if total - largest >= count - 1 else 0
    holding, spare = [largest] + [least] * (count - 1), total - largest - least * (count - 1)
    while spare > 0:
        free = [i for i in range(1, count) if holding[i] < largest] or [i for i in range(1, count) if holding[i] < bound]
        whole, remaining = sum([weights[i] for i in free]), spare
        for i in free:
            addition = min(bound - holding[i], max(1, remaining * weights[i] // whole), spare)
            holding[i] = holding[i] + addition
            spare = spare - addition
    return np.array(holding)


def setup_inputs(seed: int = 0) -> dict:
    streams_of = jax.random.split(jax.random.key(seed), 9)
    child_panel = draw_child_panel(jax.random.fold_in(streams_of[8], 71), 0)
    child_blocks = draw_child_blocks(jax.random.fold_in(streams_of[8], 71), 0)
    tile_rows = plant(jax.random.randint(streams_of[2], (N_LVL, FRONTS, N_GRID, SLOTS_DEV), 0, CHILD_LOCAL), jax.random.fold_in(streams_of[2], 1), 0, CHILD_LOCAL - 1).astype(jnp.int32)
    tile_cols = plant(jax.random.randint(streams_of[3], (N_LVL, FRONTS, N_GRID, SLOTS_DEV), 0, CHILD_SPAN), jax.random.fold_in(streams_of[3], 1), 0, CHILD_SPAN - 1).astype(jnp.int32)
    tile_parent_keys = jax.random.split(jax.random.fold_in(streams_of[4], 1), N_LVL * FRONTS * N_GRID * SLOTS_DEV // SLOTS_DEV)
    tile_parent_turns = jax.random.permutation(jax.random.fold_in(streams_of[4], 3), N_LVL * FRONTS * N_GRID * SLOTS_DEV // SLOTS_DEV)
    tile_parent = jax.vmap(lambda own, number: assign_block(jax.random.fold_in(streams_of[4], 2), own, number, SLOTS_DEV, FRONTS, 1, CAPACITY, 2))(tile_parent_keys, tile_parent_turns).reshape((N_LVL, FRONTS, N_GRID, SLOTS_DEV, 1))
    tile_place = plant(jax.random.randint(streams_of[5], (N_LVL, FRONTS, N_GRID, SLOTS_DEV), 0, PARENT_LOCAL * PARENT_SPAN), jax.random.fold_in(streams_of[5], 1), 0, (PARENT_LOCAL * PARENT_SPAN) - 1).astype(jnp.int32)
    parent_owner = jax.random.permutation(streams_of[6], FRONTS).astype(jnp.int32)
    parent_front = draw_parent_front(jax.random.fold_in(streams_of[8], 71), 0)
    return dict(child_panel=child_panel, child_blocks=child_blocks, tile_rows=tile_rows, tile_cols=tile_cols, tile_parent=tile_parent, tile_place=tile_place, parent_owner=parent_owner, parent_front=parent_front)


def reference(child_panel, child_blocks, tile_rows, tile_cols, tile_parent, tile_place, parent_owner, parent_front):
    full_panel = child_panel.reshape(FRONTS, CHILD_SPAN * BLOCK, PANEL)
    owners = parent_owner[tile_parent[..., 0]]
    level_ids = jnp.broadcast_to(jnp.arange(N_LVL, dtype=jnp.int32).reshape(N_LVL, 1, 1), (N_LVL, N_GRID, SLOTS_DEV))
    grid_ids = jnp.broadcast_to(jnp.arange(N_GRID, dtype=jnp.int32).reshape(1, N_GRID, 1), (N_LVL, N_GRID, SLOTS_DEV))
    initial = parent_front.reshape(FRONTS, PARENT_LOCAL, N_GRID, N_LVL, HALF_ROWS, PARENT_SPAN, BLOCK)

    def add_child(assembled, child_index):
        panel_rows = full_panel[child_index]
        gram_block = (-jnp.dot(panel_rows.astype(jnp.float32), panel_rows.T.astype(jnp.float32), preferred_element_type=jnp.float32)).astype(jnp.bfloat16)
        gram_block = gram_block.reshape(CHILD_SPAN, N_LVL, HALF_ROWS, CHILD_SPAN, BLOCK)
        row_block = tile_rows[:, child_index] * N_GRID + grid_ids
        col_block = tile_cols[:, child_index]
        picked = gram_block[row_block, level_ids, :, col_block, :]
        child_size = child_blocks[child_index]
        live_tile = (row_block < child_size) & (col_block < child_size)
        update_tiles = jnp.where(live_tile[..., None, None], picked, jnp.zeros((), jnp.bfloat16))
        places = tile_place[:, child_index]
        assembled = assembled.at[owners[:, child_index], places // PARENT_SPAN, grid_ids, level_ids, :, places % PARENT_SPAN, :].add(update_tiles.astype(jnp.float32))
        return (assembled, None)
    assembled, _ = lax.scan(add_child, initial, jnp.arange(FRONTS, dtype=jnp.int32))

    def factor(front_part):
        whole_front = front_part.reshape(PARENT_SPAN * BLOCK, FRONT_WIDTH)
        pivot_block = whole_front[:BLOCK, :BLOCK]
        pivot_block = 0.5 * (pivot_block + pivot_block.T)
        lower_factor = jnp.linalg.cholesky(pivot_block)
        panel_rows = lax.linalg.triangular_solve(lower_factor, whole_front[:, :BLOCK], left_side=False, lower=True, transpose_a=True)
        trailing = whole_front[:, BLOCK:] - jnp.dot(panel_rows, panel_rows[BLOCK:].T, precision=lax.Precision.HIGHEST)
        return jnp.concatenate([panel_rows, trailing], axis=1).reshape(PARENT_LOCAL, N_GRID, N_LVL, HALF_ROWS, FRONT_WIDTH)
    return lax.map(factor, assembled.reshape(FRONTS, PARENT_LOCAL, N_GRID, N_LVL, HALF_ROWS, FRONT_WIDTH))
```

```python
import functools

import jax
import jax.numpy as jnp
from jax import lax
from jax.experimental import pallas as pl
from jax.experimental.pallas import tpu as pltpu
from jax.sharding import PartitionSpec as P

BLOCK = 256
NB = 32
SUB = 8
HIGHEST = lax.Precision.HIGHEST
HIGH = lax.Precision.HIGH
NT = (((1,), (1,)), ((), ()))
TN = (((0,), (0,)), ((), ()))


def eliminate(work, inverse, begin, end):
    n = BLOCK
    row_ids = lax.broadcasted_iota(jnp.int32, (NB, 1), 0)

    def step(kb, carry):
        rows = work[:NB, :]
        for sub in range(NB // SUB):
            first = sub * SUB
            cols = [
                jnp.broadcast_to(rows[:, first + i : first + i + 1], (NB, 128))
                for i in range(SUB)
            ]
            for i in range(SUB):
                j = first + i
                inv = lax.rsqrt(cols[i][j : j + 1, :])
                below = jnp.where(row_ids > j, cols[i] * inv, 0.0)
                for m in range(i + 1, SUB):
                    cols[m] = cols[m] - below * (cols[m][j : j + 1, :] * inv)
                inv_wide = jnp.concatenate([inv] * (2 * n // 128), axis=1)
                below_wide = jnp.concatenate([below] * (2 * n // 128), axis=1)
                urow = rows[j : j + 1, :] * inv_wide
                rows = jnp.where(row_ids == j, urow, rows - below_wide * urow)
        at = pl.ds(pl.multiple_of(kb * NB, NB), NB)
        inverse[at, :] = pltpu.roll(rows, kb * NB + n, 1)[:, :n]
        update = lax.dot_general(
            rows[:, :n], rows, TN, precision=HIGHEST, preferred_element_type=jnp.float32
        )
        rest = work[NB:, :] - update[NB:, :]
        work[: n - NB, :] = pltpu.roll(rest, 2 * n - NB, 1)
        return carry

    lax.fori_loop(begin, end, step, 0)


def schur_kernel(acc, inverse, shared, out, block, sems):
    local, half, width = acc.shape
    grids, levels = shared.shape[0], shared.shape[1]
    blocks = width // BLOCK

    def put(b):
        lanes = pl.ds(pl.multiple_of(b * BLOCK, BLOCK), BLOCK)
        return pltpu.make_async_copy(block.at[b], out.at[:, :, lanes], sems.at[b])

    column = acc[:, :, :BLOCK].reshape(local * half, BLOCK)
    rows = lax.dot_general(
        column, inverse[...], NT, precision=HIGHEST, preferred_element_type=jnp.float32
    )
    block[0] = rows.reshape(local, half, BLOCK)
    put(0).start()
    weights = jnp.dot(rows, inverse[...], precision=HIGHEST, preferred_element_type=jnp.float32)
    for b in range(1, blocks):
        g, s = b % grids, b // grids
        other = shared[g, :, s].reshape(levels * half, BLOCK)
        prod = lax.dot_general(
            weights, other, NT, precision=HIGH, preferred_element_type=jnp.float32
        ).reshape(local, half, BLOCK)
        block[b] = acc[:, :, b * BLOCK : (b + 1) * BLOCK] - prod
        put(b).start()
    for b in range(blocks):
        put(b).wait()


class Sends:
    def __init__(self, send_sems, recv_sems, first_send=0, first_recv=0):
        self.send_sems, self.recv_sems, self.started = send_sems, recv_sems, []
        self.first_send, self.first_recv, self.used = first_send, first_recv, 0

    def make(self, src, dst, device):
        copy = pltpu.make_async_remote_copy(
            src_ref=src,
            dst_ref=dst,
            send_sem=self.send_sems.at[self.first_send + self.used],
            recv_sem=self.recv_sems.at[self.first_recv + self.used],
            device_id=device,
            device_id_type=pl.DeviceIdType.MESH,
        )
        self.used += 1
        return copy

    def start(self, src, dst, device):
        copy = self.make(src, dst, device)
        copy.start()
        self.started.append(copy)
        return copy

    def finish(self):
        for copy in self.started:
            copy.wait_send()


def greet(devices):
    barrier = pltpu.get_barrier_semaphore()
    for device in devices:
        pl.semaphore_signal(barrier, inc=1, device_id=device, device_id_type=pl.DeviceIdType.MESH)
    pl.semaphore_wait(barrier, len(devices))


def plane_peers():
    level, grid = lax.axis_index("lvl"), lax.axis_index("grid")
    across = grid + 1 - 2 * (grid % 2)
    along = (grid + 2) % 4
    return level, grid, across, along


def share_kernel(own, pivot, out, inverse, work, send_sems, recv_sems, local_sem):
    level, grid, across, along = plane_peers()
    greet([{"grid": across}, {"grid": along}, {"lvl": 1 - level}])
    share_body(own, lambda: pivot[...], out, inverse, work, Sends(send_sems, recv_sems), local_sem)


def share_body(own, whole_pivot, out, inverse, work, sends, local_sem):
    level, grid, across, along = plane_peers()
    corner = (across + 2) % 4
    x_peer, y_peer, core = {"grid": across}, {"grid": along}, {"lvl": 1 - level}
    local = out.shape[2]
    mine = pltpu.make_async_copy(own, out.at[grid, level], local_sem)
    to_x = [None] * local
    to_y = [None] * local
    to_core = []
    for r in range(local):
        place = out.at[grid, level, r]
        to_x[r] = sends.start(own.at[r], place, x_peer)
        place = out.at[grid, level, local - 1 - r]
        to_y[local - 1 - r] = sends.start(own.at[local - 1 - r], place, y_peer)
    to_core.append(sends.start(own, out.at[grid, level], core))
    mine.start()
    whole = whole_pivot()
    work[:, :BLOCK] = 0.5 * (whole + whole.T)
    work[:, BLOCK:] = (
        lax.broadcasted_iota(jnp.int32, (BLOCK, BLOCK), 0)
        == lax.broadcasted_iota(jnp.int32, (BLOCK, BLOCK), 1)
    ).astype(jnp.float32)
    eliminate(work, inverse, 0, 5)
    to_x[0].wait_recv()
    half = out.at[across, level, 0]
    corner_y = sends.start(half, half, y_peer)
    to_y[1].wait_recv()
    half = out.at[along, level, 1]
    corner_x = sends.start(half, half, x_peer)
    for r in range(1, local):
        to_x[r].wait_recv()
    place = out.at[across, level]
    to_core.append(sends.start(place, place, core))
    to_y[0].wait_recv()
    place = out.at[along, level]
    to_core.append(sends.start(place, place, core))
    eliminate(work, inverse, 5, BLOCK // NB)
    corner_y.wait_recv()
    half = out.at[corner, level, 0]
    to_core.append(sends.start(half, half, core))
    corner_x.wait_recv()
    half = out.at[corner, level, 1]
    to_core.append(sends.start(half, half, core))
    mine.wait()
    for copy in to_core:
        copy.wait_recv()
    sends.finish()


ALL_FRONTS = 4
TURNS = (
    (0, 0), (0, 1), (0, 2), (1, 0), (0, 3), (2, 0), (1, 1), (1, 2),
    (3, 0), (2, 1), (2, 2), (2, 3), (1, 3), (3, 1), (3, 2), (3, 3),
)
BEFORE = (0, 1, 3, 5, 7, 8, 10, 13, 14)
BETWEEN = (4, 11, 12)
ROWS = 16
Z, ZC, XH, YH, CX, CY, CORE, META, PIVOT_META, RAW = 0, 4, 8, 16, 24, 28, 32, 48, 52, 54
SHARE = 58


def choose(index, values):
    out = jnp.int32(values[0])
    for i in range(1, len(values)):
        out = jnp.where(index == i, values[i], out)
    return out


def assemble_kernel(
    own, tile_rows, tile_cols, tile_parent, tile_place, child_blocks, parent_owner, parent,
    acc, shared, inverse,
    fields, codes, panels, met, pivot_met, counts, pivot_counts, tiles, raw, pivot, work,
    send_sems, recv_sems, local_sems,
):
    level, grid, across, along = plane_peers()
    corner = (across + 2) % 4
    front = lax.axis_index("front")
    pair, inner = front + 1 - 2 * (front % 2), 3 - front
    turn = [front, pair, 2 - front // 2, 3 - 3 * (front // 2)]
    middle = (front == 1) | (front == 2)
    local, half, depth = own.shape
    levels, grids = panels.shape[2], panels.shape[1]
    spots = acc.shape[0] * acc.shape[2] // BLOCK
    width_blocks = acc.shape[2] // BLOCK
    pieces = local * local
    x_peer, y_peer, core = {"grid": across}, {"grid": along}, {"lvl": 1 - level}
    fronts = [{"front": pair}, {"front": (front + 2) % 4}, {"front": inner}]
    plane = [x_peer, y_peer, {"grid": corner}]

    used = [0]
    finish = []

    def remote(src, dst, recv, device, when=None):
        copy = pltpu.make_async_remote_copy(
            src_ref=src,
            dst_ref=dst,
            send_sem=send_sems.at[used[0]],
            recv_sem=recv_sems.at[recv],
            device_id=device,
            device_id_type=pl.DeviceIdType.MESH,
        )
        used[0] += 1
        finish.append((when, copy))
        return copy

    def at(k, g, lv=level):
        return panels.at[turn[k], g, lv]

    parent_in = pltpu.make_async_copy(parent, acc, local_sems.at[0])
    own_in = pltpu.make_async_copy(own, at(0, grid), local_sems.at[1])
    fields_in = [
        pltpu.make_async_copy(ref, fields.at[i], local_sems.at[5 + i])
        for i, ref in enumerate((tile_rows, tile_cols, tile_parent, tile_place))
    ]
    for copy in fields_in + [own_in, parent_in]:
        copy.start()

    met_out = [remote(codes, met.at[front], META + front, d) for d in fronts]
    z_own = remote(own, at(0, grid), Z + front, {"front": pair})
    z_own_in = remote(own, at(0, grid), Z + front, {"front": inner}, middle)
    z_on = [None] + [
        remote(at(k, grid), at(k, grid), Z + turn[k], {"front": to}, middle)
        for k, to in ((1, inner), (2, pair), (3, pair))
    ]
    zc_own = remote(at(0, corner), at(0, corner), ZC + front, {"front": pair})
    to_x, to_y, to_core, on_x, on_y = [], [], [], {}, {}
    for k in range(4):
        mine = own if k == 0 else at(k, grid)
        to_x.append([remote(mine.at[h], at(k, grid).at[h], XH + 2 * k + h, x_peer) for h in (0, 1)])
        to_y.append([remote(mine.at[h], at(k, grid).at[h], YH + 2 * k + h, y_peer) for h in (0, 1)])
        sources = [mine, at(k, across), at(k, along), at(k, corner)]
        to_core.append([
            remote(source, at(k, g), CORE + 4 * k + p, core)
            for p, (source, g) in enumerate(zip(sources, (grid, across, along, corner)))
        ])
        if k != 1:
            x_half, y_half = at(k, across).at[0], at(k, along).at[1]
            on_y[k] = remote(x_half, x_half, CY + k, y_peer)
            on_x[k] = remote(y_half, y_half, CX + k, x_peer)
    is_first = grid == 0
    pivot_meta = [remote(met, pivot_met, PIVOT_META, d, is_first) for d in plane]
    met_in = pltpu.make_async_copy(met, pivot_met, local_sems.at[2])
    first = parent.at[0, :, pl.ds(0, BLOCK)]
    raw_x = remote(first, raw, RAW, x_peer, is_first)
    raw_y = remote(first, raw, RAW, y_peer, is_first)
    raw_in = pltpu.make_async_copy(first, raw, local_sems.at[3])
    raw_halves = [raw.at[pl.ds(h * (half // 2), half // 2)] for h in (0, 1)]
    raw_on = [
        remote(raw_halves[0], raw_halves[0], RAW + 1, y_peer, grid == 1),
        remote(raw_halves[1], raw_halves[1], RAW + 2, x_peer, grid == 2),
    ]
    pivot_core = remote(pivot.at[level], pivot.at[level], RAW + 3, core)

    for copy in fields_in:
        copy.wait()
    row, col, named, spot = [fields[i] for i in range(4)]
    live = (row * grids + grid < child_blocks[0]) & (col < child_blocks[0])
    owner = jnp.zeros_like(named)
    for q in range(ALL_FRONTS):
        owner = jnp.where(named == q, parent_owner[q], owner)
    code = (col % grids) * (spots * pieces) + spot * pieces + row * local + col // grids
    code = jnp.where(live, code, -1)
    ids = lax.broadcasted_iota(jnp.int32, codes.shape, 0)
    codes[...] = jnp.where(owner == ids, code, -1)
    met[pl.ds(front, 1)] = codes[...][None]
    greet(fronts + plane + [core])

    def spread(k):
        to_x[k][0].start()
        to_y[k][1].start()
        to_core[k][0].start()
        to_x[k][1].start()
        to_y[k][0].start()

    z_own.start()

    @pl.when(middle)
    def _():
        z_own_in.start()

    for copy in met_out:
        copy.start()
    spread(0)

    def pass_on(k):
        z_on_wait(k)
        z_on[k].start()

    def z_on_wait(k):
        pltpu.make_async_remote_copy(
            src_ref=at(k, grid), dst_ref=at(k, grid), send_sem=send_sems.at[0],
            recv_sem=recv_sems.at[Z + turn[k]], device_id=core, device_id_type=pl.DeviceIdType.MESH,
        ).wait_recv()

    def zc_wait(k):
        pltpu.make_async_remote_copy(
            src_ref=at(k, corner), dst_ref=at(k, corner), send_sem=send_sems.at[0],
            recv_sem=recv_sems.at[ZC + turn[k]], device_id=core, device_id_type=pl.DeviceIdType.MESH,
        ).wait_recv()

    def relay(k):
        to_x[k][0].wait_recv()
        on_y[k].start()
        to_y[k][1].wait_recv()
        on_x[k].start()

    def x_in(k):
        to_x[k][1].wait_recv()
        to_core[k][1].start()

    def y_in(k):
        to_y[k][0].wait_recv()
        to_core[k][2].start()

    def corner_in(k):
        on_x[k].wait_recv()
        on_y[k].wait_recv()
        to_core[k][3].start()

    def end_in(k):
        @pl.when(jnp.logical_not(middle))
        def _():
            z_on_wait(k)

    def before(i):
        if i == 0:
            own_in.wait()
            parent_in.wait()
        elif i == 1:
            relay(0)
            x_in(0)

            @pl.when(middle)
            def _():
                pass_on(1)
                pass_on(2)

            end_in(1)
            spread(1)
            y_in(0)
        elif i == 3:
            corner_in(0)
            for d in range(3):
                pltpu.make_async_remote_copy(
                    src_ref=codes, dst_ref=met.at[0], send_sem=send_sems.at[0],
                    recv_sem=recv_sems.at[META + (front + d + 1) % 4], device_id=core,
                    device_id_type=pl.DeviceIdType.MESH,
                ).wait_recv()

            @pl.when(is_first)
            def _():
                met_in.start()
                raw_in.start()
                for copy in pivot_meta:
                    copy.start()
                met_in.wait()
                raw_in.wait()
        elif i == 5:
            to_x[1][0].wait_recv()
            to_y[1][1].wait_recv()
            x_in(1)
            y_in(1)
        elif i == 7:
            relay(2)
        elif i == 8:
            end_in(3)
            spread(3)
            x_in(2)
            y_in(2)
            for g in (1, 2):

                @pl.when(grid == g)
                def _(g=g):
                    raw_x.wait_recv()
                    raw_on[g - 1].start()
        elif i == 10:
            corner_in(2)
        elif i == 13:

            @pl.when(grid == 3)
            def _():
                raw_on[0].wait_recv()
                raw_on[1].wait_recv()
        elif i == 14:
            corner_in(3)

    def between(i):
        if i == 4:

            @pl.when(middle)
            def _():
                pass_on(3)

            zc_own.start()
            end_in(2)
            spread(2)

            @pl.when(is_first)
            def _():
                raw_x.start()
                raw_y.start()

            @pl.when(jnp.logical_not(is_first))
            def _():
                pivot_meta[0].wait_recv()
        elif i == 11:
            zc_wait(1)
            to_core[1][3].start()
        elif i == 12:
            relay(3)
            x_in(3)
            y_in(3)

    def expand(k, c):
        row = met[c, pl.ds(front, 1), :]
        ones = jnp.ones((row.shape[1], 128), jnp.bfloat16)
        ids = lax.broadcasted_iota(jnp.int32, (grids * spots * pieces, row.shape[1]), 0)
        hit = jnp.where(ids == row, 1.0, 0.0).astype(jnp.bfloat16)
        count = jnp.dot(hit, ones, preferred_element_type=jnp.float32)
        counts[k] = jnp.broadcast_to(
            count.reshape(grids, spots * pieces, 1, 128), (grids, spots * pieces, 8, 128)
        )

    def expand_pivot(c):
        row = pivot_met[c, pl.ds(front, 1), :]
        ones = jnp.ones((row.shape[1], 128), jnp.bfloat16)
        ids = lax.broadcasted_iota(jnp.int32, (grids * pieces, row.shape[1]), 0)
        ids = (ids // pieces) * (spots * pieces) + ids % pieces
        hit = jnp.where(ids == row, 1.0, 0.0).astype(jnp.bfloat16)
        count = jnp.dot(hit, ones, preferred_element_type=jnp.float32)
        pivot_counts[...] = jnp.broadcast_to(
            count.reshape(grids * pieces, 1, 128), (grids * pieces, 8, 128)
        )

    def pick(ref, first, lane):
        value = ref[pl.ds(pl.multiple_of(first, ROWS), ROWS), lane : lane + half]
        return value.astype(jnp.float32).reshape(ROWS // 8, 8, half)

    def multiply(k, c, g):
        right = panels[c, g].reshape(levels * local * half, depth)
        left = panels[c, grid, level].reshape(local * half, depth)
        prod = lax.dot_general(left, right, NT, preferred_element_type=jnp.float32)
        tiles[...] = (-prod).astype(jnp.bfloat16)

        def add(i, carry):
            rows = pl.ds(pl.multiple_of(i * ROWS, ROWS), ROWS)
            parts = [
                [
                    pick(tiles, r * half + i * ROWS, (m * local + s) * half)
                    for r in range(local)
                    for s in range(local)
                ]
                for m in range(levels)
            ]
            for p in range(spots):
                lane = p % width_blocks * BLOCK
                many = [counts[k, g, p * pieces + x][None] for x in range(pieces)]
                for m in range(levels):
                    at = slice(lane + m * half, lane + (m + 1) * half)
                    total = acc[p // width_blocks, rows, at].reshape(ROWS // 8, 8, half)
                    for x in range(pieces):
                        total = total + many[x] * parts[m][x]
                    acc[p // width_blocks, rows, at] = total.reshape(ROWS, half)
            return carry

        lax.fori_loop(0, half // ROWS, add, 0)

    def multiply_pivot(c):
        expand_pivot(c)

        def of(g, carry):
            right = panels[c, g].reshape(levels * local * half, depth)
            left = panels[c, 0, level].reshape(local * half, depth)
            prod = lax.dot_general(left, right, NT, preferred_element_type=jnp.float32)
            tiles[...] = (-prod).astype(jnp.bfloat16)

            def add(i, inside):
                rows = pl.ds(pl.multiple_of(i * ROWS, ROWS), ROWS)
                for m in range(levels):
                    at = slice(m * half, (m + 1) * half)
                    total = pivot[level, rows, at].reshape(ROWS // 8, 8, half)
                    for r in range(local):
                        for s in range(local):
                            part = pick(tiles, r * half + i * ROWS, (m * local + s) * half)
                            many = pivot_counts[g * pieces + r * local + s]
                            total = total + many[None] * part
                    pivot[level, rows, at] = total.reshape(ROWS, half)
                return inside

            lax.fori_loop(0, half // ROWS, add, 0, unroll=4)
            return carry

        lax.fori_loop(0, grids, of, 0)

    pivot[level] = jnp.zeros_like(pivot[level])

    def step(i, carry):
        for j in range(len(TURNS)):
            if j in BEFORE:

                @pl.when(i == j)
                def _(j=j):
                    before(j)

        k = choose(i, [t[0] for t in TURNS])
        p = choose(i, [t[1] for t in TURNS])
        c = choose(k, turn)
        g = choose(p, [grid, across, along, corner])
        pltpu.make_async_remote_copy(
            src_ref=panels.at[c, g, level], dst_ref=panels.at[c, g, level],
            send_sem=send_sems.at[0], recv_sem=recv_sems.at[CORE + 4 * k + p],
            device_id=core, device_id_type=pl.DeviceIdType.MESH,
        ).wait_recv()

        @pl.when(p == 0)
        def _():
            expand(k, c)

        multiply(k, c, g)
        for j in BETWEEN:

            @pl.when(i == j)
            def _(j=j):
                between(j)

        @pl.when(p == 3)
        def _():
            multiply_pivot(c)

        return carry

    lax.fori_loop(0, len(TURNS), step, 0)

    pivot[level] = pivot[level] + raw[...]
    pivot_core.start()

    def whole():
        pivot_core.wait_recv()
        return pivot[...].reshape(BLOCK, BLOCK)

    share_body(
        acc.at[:, :, pl.ds(0, BLOCK)], whole, shared, inverse, work,
        Sends(send_sems, recv_sems, used[0], SHARE), local_sems.at[4],
    )
    for when, copy in finish:
        if when is None:
            copy.wait_send()
        else:

            @pl.when(when)
            def _(copy=copy):
                copy.wait_send()


VMEM = pl.BlockSpec(memory_space=pltpu.VMEM)
HBM = pl.BlockSpec(memory_space=pltpu.HBM)
ANY = pl.BlockSpec(memory_space=pl.ANY)
SMEM = pl.BlockSpec(memory_space=pltpu.SMEM)


def owner_of(parents, parent_owner):
    ids = jnp.arange(parent_owner.shape[0], dtype=jnp.int32)
    return jnp.sum(jnp.where(parents[..., None] == ids, parent_owner, 0), axis=-1)


def assemble_all(
    child_panel, child_blocks, tile_rows, tile_cols, tile_parent, tile_place, parent_owner, parent_front
):
    levels, grids, fronts = lax.axis_size("lvl"), lax.axis_size("grid"), lax.axis_size("front")
    local, half, depth = child_panel.shape[1], child_panel.shape[4], child_panel.shape[5]
    parent_local, width = parent_front.shape[1], parent_front.shape[5]
    slots = tile_rows.shape[3]
    spots = parent_local * width // BLOCK
    pieces = local * local
    parent = parent_front.reshape(parent_local, half, width)
    sends = 100
    return pl.pallas_call(
        assemble_kernel,
        out_shape=(
            jax.ShapeDtypeStruct(parent.shape, jnp.float32),
            jax.ShapeDtypeStruct((grids, levels, parent_local, half, BLOCK), jnp.float32),
            jax.ShapeDtypeStruct((BLOCK, BLOCK), jnp.float32),
        ),
        in_specs=[HBM] * 5 + [SMEM, SMEM, HBM],
        out_specs=(VMEM, VMEM, VMEM),
        scratch_shapes=[
            pltpu.VMEM((4, 1, slots), jnp.int32),
            pltpu.VMEM((8, slots), jnp.int32),
            pltpu.VMEM((fronts, grids, levels, local, half, depth), jnp.bfloat16),
            pltpu.VMEM((fronts, 8, slots), jnp.int32),
            pltpu.VMEM((fronts, 8, slots), jnp.int32),
            pltpu.VMEM((fronts, grids, spots * pieces, 8, 128), jnp.float32),
            pltpu.VMEM((grids * pieces, 8, 128), jnp.float32),
            pltpu.VMEM((local * half, levels * local * half), jnp.bfloat16),
            pltpu.VMEM((half, BLOCK), jnp.float32),
            pltpu.VMEM((levels, half, BLOCK), jnp.float32),
            pltpu.VMEM((BLOCK, 2 * BLOCK), jnp.float32),
            pltpu.SemaphoreType.DMA((sends,)),
            pltpu.SemaphoreType.DMA((SHARE + 12,)),
            pltpu.SemaphoreType.DMA((9,)),
        ],
        compiler_params=pltpu.CompilerParams(
            collective_id=0, has_side_effects=True, vmem_limit_bytes=48 * 1024 * 1024
        ),
        name="assemble",
    )(
        child_panel.reshape(local, half, depth),
        *(a.reshape(1, slots) for a in (tile_rows, tile_cols, tile_parent, tile_place)),
        child_blocks,
        parent_owner,
        parent,
    )


def exchange_tiles(
    child_panel, child_blocks, tile_rows, tile_cols, tile_parent, tile_place, parent_owner, parent_front
):
    levels, grids, fronts = lax.axis_size("lvl"), lax.axis_size("grid"), lax.axis_size("front")
    grid_index = lax.axis_index("grid")
    local, half, depth = child_panel.shape[1], child_panel.shape[4], child_panel.shape[5]
    parent_local, width = parent_front.shape[1], parent_front.shape[5]
    slots = tile_rows.shape[3]
    blocks = width // BLOCK
    capacity = 2 * slots // fronts
    own = child_panel.reshape(local * half, depth)
    view = lax.all_gather(
        own.reshape(1, local, half, depth), ("grid", "lvl"), axis=0, tiled=True
    ).reshape(grids, levels, local, half, depth)
    gram = jnp.einsum("ik,glsjk->isglj", own, view, preferred_element_type=jnp.float32)
    gram = (-gram).astype(jnp.bfloat16).reshape(local, half, local * grids, BLOCK)
    gram = gram.transpose(0, 2, 1, 3).reshape(local * local * grids, half, BLOCK)
    row, col = tile_rows.reshape(slots), tile_cols.reshape(slots)
    live = (row * grids + grid_index < child_blocks[0]) & (col < child_blocks[0])
    owners = owner_of(tile_parent.reshape(slots), parent_owner)
    before = (jnp.arange(slots)[:, None] > jnp.arange(slots)[None, :]).astype(jnp.int32)
    same = (owners[:, None] == owners[None, :]).astype(jnp.int32)
    rank = jnp.sum(before * same, axis=1)
    index = owners * capacity + rank
    matches = index[None, :] == jnp.arange(fronts * capacity, dtype=jnp.int32)[:, None]
    filled = jnp.any(matches & live[None, :], axis=1)
    spans = local * grids
    pick = (row * spans + col)[:, None] == jnp.arange(local * spans, dtype=jnp.int32)[None, :]
    pick = jnp.any((matches & live[None, :])[:, :, None] & pick[None], axis=1)
    place = jnp.sum(jnp.where(matches, tile_place.reshape(slots)[None, :], 0), axis=1)
    outgoing = jnp.einsum(
        "kt,tij->kij", pick.astype(jnp.bfloat16), gram, preferred_element_type=jnp.float32
    ).astype(jnp.bfloat16)
    positions = jnp.where(filled, place, -1)
    incoming = lax.all_to_all(outgoing, "front", split_axis=0, concat_axis=0, tiled=True)
    landed = lax.all_to_all(positions, "front", split_axis=0, concat_axis=0, tiled=True)
    spots = parent_local * blocks
    selector = (landed[:, None] == jnp.arange(spots, dtype=jnp.int32)[None, :]).astype(jnp.bfloat16)
    contrib = jnp.einsum("sk,sij->kij", selector, incoming, preferred_element_type=jnp.float32)
    contrib = contrib.reshape(parent_local, blocks, half, BLOCK).transpose(0, 2, 1, 3)
    assembled = parent_front.reshape(parent_local, half, width) + contrib.reshape(
        parent_local, half, width
    )
    raw = lax.all_gather(assembled[0, :, :BLOCK][None], ("grid", "lvl"), axis=0, tiled=True)
    raw = raw[:levels].reshape(levels * half, BLOCK)
    return assembled, raw


def share_columns(assembled, pivot):
    levels, grids = lax.axis_size("lvl"), lax.axis_size("grid")
    column = assembled[:, :, :BLOCK]
    return pl.pallas_call(
        share_kernel,
        out_shape=(
            jax.ShapeDtypeStruct((grids, levels) + column.shape, jnp.float32),
            jax.ShapeDtypeStruct((BLOCK, BLOCK), jnp.float32),
        ),
        in_specs=[VMEM, VMEM],
        out_specs=(VMEM, VMEM),
        scratch_shapes=[
            pltpu.VMEM((BLOCK, 2 * BLOCK), jnp.float32),
            pltpu.SemaphoreType.DMA((12,)),
            pltpu.SemaphoreType.DMA((12,)),
            pltpu.SemaphoreType.DMA,
        ],
        compiler_params=pltpu.CompilerParams(
            collective_id=1, has_side_effects=True, vmem_limit_bytes=16 * 1024 * 1024
        ),
        name="share",
    )(column, pivot)


def per_device(*args):
    parent_front = args[-1]
    if lax.axis_size("front") == ALL_FRONTS:
        assembled, shared, inverse = assemble_all(*args)
    else:
        assembled, pivot = exchange_tiles(*args)
        shared, inverse = share_columns(assembled, pivot)
    local, half, width = assembled.shape
    result = pl.pallas_call(
        schur_kernel,
        out_shape=jax.ShapeDtypeStruct(assembled.shape, jnp.float32),
        in_specs=[VMEM, VMEM, VMEM],
        out_specs=ANY,
        scratch_shapes=[
            pltpu.VMEM((width // BLOCK, local, half, BLOCK), jnp.float32),
            pltpu.SemaphoreType.DMA((width // BLOCK,)),
        ],
        compiler_params=pltpu.CompilerParams(vmem_limit_bytes=20 * 1024 * 1024),
        name="schur",
    )(assembled, inverse, shared)
    return result.reshape(parent_front.shape)


def solution(mesh):
    return jax.shard_map(
        per_device,
        mesh=mesh,
        in_specs=(
            P("front", None, "grid", "lvl", None, None),
            P("front"),
            P("lvl", "front", "grid", None),
            P("lvl", "front", "grid", None),
            P("lvl", "front", "grid", None, None),
            P("lvl", "front", "grid", None),
            P(),
            P("front", None, "grid", "lvl", None, None),
        ),
        out_specs=P("front", None, "grid", "lvl", None, None),
        check_vma=False,
    )
```

```python
import functools

import jax
import jax.numpy as jnp
from jax import lax
from jax.experimental import pallas as pl
from jax.experimental.pallas import tpu as pltpu
from jax.sharding import PartitionSpec as P

BLOCK = 256
NB = 32
SUB = 8
HIGHEST = lax.Precision.HIGHEST
HIGH = lax.Precision.HIGH
NT = (((1,), (1,)), ((), ()))
TN = (((0,), (0,)), ((), ()))


def eliminate(work, inverse, begin, end):
    n, side = BLOCK, 128
    row_ids = lax.broadcasted_iota(jnp.int32, (NB, 1), 0)
    for kb in range(begin, end):
        first = kb * NB
        base = first // side * side
        low, high = base, base + 3 * side
        tiles = (high - low) // 128
        rows = work[first : first + NB, low:high]
        for sub in range(NB // SUB):
            at = first - low + sub * SUB
            cols = [
                jnp.broadcast_to(rows[:, at + i : at + i + 1], (NB, 128)) for i in range(SUB)
            ]
            for i in range(SUB):
                j = sub * SUB + i
                head = cols[i][j : j + 1, :]
                inv, per = lax.rsqrt(head), 1.0 / head
                for m in range(i + 1, SUB):
                    cols[m] = cols[m] - (cols[i] * cols[m][j : j + 1, :]) * per
                below = jnp.where(row_ids > j, cols[i] * inv, 0.0)
                urow = rows[j : j + 1, :] * jnp.concatenate([inv] * tiles, axis=1)
                wide = jnp.concatenate([below] * tiles, axis=1)
                rows = jnp.where(row_ids == j, urow, rows - wide * urow)
        if base == 0:
            inverse[first : first + NB, :side] = rows[:, n:high]
            inverse[first : first + NB, side:] = jnp.zeros((NB, n - side), jnp.float32)
        else:
            inverse[first : first + NB, :] = rows[:, n - low :]
        if first + NB < base + side:
            update = lax.dot_general(
                rows[:, :side], rows, TN, precision=HIGHEST, preferred_element_type=jnp.float32
            )
            work[first + NB : base + side, low:high] = (
                work[first + NB : base + side, low:high] - update[first + NB - base :, :]
            )
        if base == 0:
            work[first : first + NB, low:high] = rows
        if first + NB == side:
            update = lax.dot_general(
                work[:side, side:n],
                work[:side, side : n + side],
                TN,
                precision=HIGHEST,
                preferred_element_type=jnp.float32,
            )
            work[side:, side : n + side] = work[side:, side : n + side] - update


def schur_kernel(acc, inverse, shared, out, block, sems):
    local, half, width = acc.shape
    grids, levels = shared.shape[0], shared.shape[1]
    blocks = width // BLOCK

    def put(b):
        lanes = pl.ds(pl.multiple_of(b * BLOCK, BLOCK), BLOCK)
        return pltpu.make_async_copy(block.at[b], out.at[:, :, lanes], sems.at[b])

    column = acc[:, :, :BLOCK].reshape(local * half, BLOCK)
    rows = lax.dot_general(
        column, inverse[...], NT, precision=HIGHEST, preferred_element_type=jnp.float32
    )
    block[0] = rows.reshape(local, half, BLOCK)
    put(0).start()
    weights = jnp.dot(rows, inverse[...], precision=HIGHEST, preferred_element_type=jnp.float32)
    for b in range(1, blocks):
        g, s = b % grids, b // grids
        other = shared[g, :, s].reshape(levels * half, BLOCK)
        prod = lax.dot_general(
            weights, other, NT, precision=HIGH, preferred_element_type=jnp.float32
        ).reshape(local, half, BLOCK)
        block[b] = acc[:, :, b * BLOCK : (b + 1) * BLOCK] - prod
        put(b).start()
    for b in range(blocks):
        put(b).wait()


class Sends:
    def __init__(self, send_sems, recv_sems, first_send=0, first_recv=0):
        self.send_sems, self.recv_sems, self.started = send_sems, recv_sems, []
        self.first_send, self.first_recv, self.used = first_send, first_recv, 0

    def make(self, src, dst, device):
        copy = pltpu.make_async_remote_copy(
            src_ref=src,
            dst_ref=dst,
            send_sem=self.send_sems.at[self.first_send + self.used],
            recv_sem=self.recv_sems.at[self.first_recv + self.used],
            device_id=device,
            device_id_type=pl.DeviceIdType.MESH,
        )
        self.used += 1
        return copy

    def start(self, src, dst, device):
        copy = self.make(src, dst, device)
        copy.start()
        self.started.append(copy)
        return copy

    def finish(self):
        for copy in self.started:
            copy.wait_send()


def greet(devices):
    barrier = pltpu.get_barrier_semaphore()
    for device in devices:
        pl.semaphore_signal(barrier, inc=1, device_id=device, device_id_type=pl.DeviceIdType.MESH)
    pl.semaphore_wait(barrier, len(devices))


def plane_peers():
    level, grid = lax.axis_index("lvl"), lax.axis_index("grid")
    across = grid + 1 - 2 * (grid % 2)
    along = (grid + 2) % 4
    return level, grid, across, along


def share_kernel(own, pivot, out, inverse, work, send_sems, recv_sems, local_sem):
    level, grid, across, along = plane_peers()
    greet([{"grid": across}, {"grid": along}, {"lvl": 1 - level}])
    share_body(own, lambda: pivot[...], out, inverse, work, Sends(send_sems, recv_sems), local_sem)


def share_body(own, whole_pivot, out, inverse, work, sends, local_sem):
    level, grid, across, along = plane_peers()
    corner = (across + 2) % 4
    x_peer, y_peer, core = {"grid": across}, {"grid": along}, {"lvl": 1 - level}
    local = out.shape[2]
    mine = pltpu.make_async_copy(own, out.at[grid, level], local_sem)
    to_x = [None] * local
    to_y = [None] * local
    to_core = []
    for r in range(local):
        place = out.at[grid, level, r]
        to_x[r] = sends.start(own.at[r], place, x_peer)
        place = out.at[grid, level, local - 1 - r]
        to_y[local - 1 - r] = sends.start(own.at[local - 1 - r], place, y_peer)
    to_core.append(sends.start(own, out.at[grid, level], core))
    mine.start()
    whole = whole_pivot()
    work[:, :BLOCK] = 0.5 * (whole + whole.T)
    work[:, BLOCK:] = (
        lax.broadcasted_iota(jnp.int32, (BLOCK, BLOCK), 0)
        == lax.broadcasted_iota(jnp.int32, (BLOCK, BLOCK), 1)
    ).astype(jnp.float32)
    eliminate(work, inverse, 0, 4)
    to_x[0].wait_recv()
    half = out.at[across, level, 0]
    corner_y = sends.start(half, half, y_peer)
    to_y[1].wait_recv()
    half = out.at[along, level, 1]
    corner_x = sends.start(half, half, x_peer)
    for r in range(1, local):
        to_x[r].wait_recv()
    place = out.at[across, level]
    to_core.append(sends.start(place, place, core))
    to_y[0].wait_recv()
    place = out.at[along, level]
    to_core.append(sends.start(place, place, core))
    eliminate(work, inverse, 4, BLOCK // NB)
    corner_y.wait_recv()
    half = out.at[corner, level, 0]
    to_core.append(sends.start(half, half, core))
    corner_x.wait_recv()
    half = out.at[corner, level, 1]
    to_core.append(sends.start(half, half, core))
    mine.wait()
    for copy in to_core:
        copy.wait_recv()
    sends.finish()


ALL_FRONTS = 4
TURNS = (
    (0, 0), (0, 1), (0, 2), (1, 0), (0, 3), (2, 0), (1, 1), (1, 2),
    (3, 0), (2, 1), (2, 2), (2, 3), (1, 3), (3, 1), (3, 2), (3, 3),
)
BEFORE = (0, 1, 3, 5, 7, 8, 10, 12, 14)
BETWEEN = (4, 11, 12)
ROWS = 16
Z, ZC, XH, YH, CX, CY, CORE, META, PART, RAW = 0, 4, 8, 16, 24, 28, 32, 48, 52, 56
SHARE = 60


def choose(index, values):
    out = jnp.int32(values[0])
    for i in range(1, len(values)):
        out = jnp.where(index == i, values[i], out)
    return out


def assemble_kernel(
    own, fields, parent,
    acc, shared, inverse,
    codes, panels, met, counts, part_counts, tiles, parts_out, parts_in, pivot, work,
    send_sems, recv_sems, local_sems,
):
    level, grid, across, along = plane_peers()
    corner = (across + 2) % 4
    front = lax.axis_index("front")
    pair, inner = front + 1 - 2 * (front % 2), 3 - front
    turn = [front, pair, 2 - front // 2, 3 - 3 * (front // 2)]
    middle = (front == 1) | (front == 2)
    local, half, depth = own.shape
    levels, grids = panels.shape[2], panels.shape[1]
    spots = acc.shape[0] * acc.shape[2] // BLOCK
    width_blocks = acc.shape[2] // BLOCK
    pieces = local * local
    x_peer, y_peer, core = {"grid": across}, {"grid": along}, {"lvl": 1 - level}
    fronts = [{"front": pair}, {"front": (front + 2) % 4}, {"front": inner}]
    plane = [x_peer, y_peer, {"grid": corner}]

    used = [0]
    finish = []

    def remote(src, dst, recv, device, when=None):
        copy = pltpu.make_async_remote_copy(
            src_ref=src,
            dst_ref=dst,
            send_sem=send_sems.at[used[0]],
            recv_sem=recv_sems.at[recv],
            device_id=device,
            device_id_type=pl.DeviceIdType.MESH,
        )
        used[0] += 1
        finish.append((when, copy))
        return copy

    def at(k, g, lv=level):
        return panels.at[turn[k], g, lv]

    parent_in = pltpu.make_async_copy(parent, acc, local_sems.at[0])
    own_in = pltpu.make_async_copy(own, at(0, grid), local_sems.at[1])
    for copy in [own_in, parent_in]:
        copy.start()

    met_out = [remote(codes, met.at[front], META + front, d) for d in fronts]
    z_own = remote(own, at(0, grid), Z + front, {"front": pair})
    z_own_in = remote(own, at(0, grid), Z + front, {"front": inner}, middle)
    z_on = [None] + [
        remote(at(k, grid), at(k, grid), Z + turn[k], {"front": to}, middle)
        for k, to in ((1, inner), (2, pair), (3, pair))
    ]
    by_z = jnp.logical_not(middle & (grid == 0))
    to_z = jnp.logical_not(jnp.logical_not(middle) & (grid == 0))
    zc_own = remote(at(0, corner), at(0, corner), ZC + front, {"front": pair}, by_z)
    to_x, to_y, to_core, on_x, on_y = [], [], [], {}, {}
    for k in range(4):
        mine = own if k == 0 else at(k, grid)
        to_x.append([remote(mine.at[h], at(k, grid).at[h], XH + 2 * k + h, x_peer) for h in (0, 1)])
        to_y.append([remote(mine.at[h], at(k, grid).at[h], YH + 2 * k + h, y_peer) for h in (0, 1)])
        sources = [mine, at(k, across), at(k, along), at(k, corner)]
        to_core.append([
            remote(source, at(k, g), CORE + 4 * k + p, core)
            for p, (source, g) in enumerate(zip(sources, (grid, across, along, corner)))
        ])
        x_half, y_half = at(k, across).at[0], at(k, along).at[1]
        by_y, by_x = None, None
        if k == 1:
            by_y = jnp.logical_not(middle) & (grid == 2)
            by_x = jnp.logical_not(middle) & (grid == 1)
        on_y[k] = remote(x_half, x_half, CY + k, y_peer, by_y)
        on_x[k] = remote(y_half, y_half, CX + k, x_peer, by_x)
    is_first = grid == 0
    part_out = [
        remote(parts_out.at[q], parts_in.at[front], PART + front, d, is_first)
        for q, d in zip((pair, (front + 2) % 4, inner), fronts)
    ]
    rows = pivot.at[level]
    raw_x = remote(rows, rows, RAW, x_peer, is_first)
    raw_y = remote(rows, rows, RAW, y_peer, is_first)
    raw_in = pltpu.make_async_copy(parent.at[0, :, pl.ds(0, BLOCK)], rows, local_sems.at[3])
    raw_halves = [pivot.at[level, pl.ds(h * (half // 2), half // 2)] for h in (0, 1)]
    raw_on = [
        remote(raw_halves[0], raw_halves[0], RAW + 1, y_peer, grid == 1),
        remote(raw_halves[1], raw_halves[1], RAW + 2, x_peer, grid == 2),
    ]
    pivot_core = remote(rows, rows, RAW + 3, core)

    slots = codes.shape[1]
    row, col, named, spot = [
        fields[i : i + 1, j * slots : (j + 1) * slots] for i in (0, 1) for j in (0, 1)
    ]
    blocks = fields[2:3, ALL_FRONTS : ALL_FRONTS + 1]
    live = (row * grids + grid < blocks) & (col < blocks)
    owner = jnp.zeros_like(named)
    for q in range(ALL_FRONTS):
        owner = jnp.where(named == q, fields[2:3, q : q + 1], owner)
    code = (col % grids) * (spots * pieces) + spot * pieces + row * local + col // grids
    code = jnp.where(live, code, -1)
    ids = lax.broadcasted_iota(jnp.int32, codes.shape, 0)
    codes[...] = jnp.where(owner == ids, code, -1)
    met[pl.ds(front, 1)] = codes[...][None]
    greet(fronts + plane + [core])

    def spread(k):
        to_x[k][0].start()
        to_y[k][1].start()
        to_core[k][0].start()
        to_x[k][1].start()
        to_y[k][0].start()

    z_own.start()

    @pl.when(middle)
    def _():
        z_own_in.start()

    for copy in met_out:
        copy.start()
    spread(0)

    def pass_on(k):
        z_on_wait(k)
        z_on[k].start()

    def z_on_wait(k):
        pltpu.make_async_remote_copy(
            src_ref=at(k, grid), dst_ref=at(k, grid), send_sem=send_sems.at[0],
            recv_sem=recv_sems.at[Z + turn[k]], device_id=core, device_id_type=pl.DeviceIdType.MESH,
        ).wait_recv()

    def zc_wait(k):
        pltpu.make_async_remote_copy(
            src_ref=at(k, corner), dst_ref=at(k, corner), send_sem=send_sems.at[0],
            recv_sem=recv_sems.at[ZC + turn[k]], device_id=core, device_id_type=pl.DeviceIdType.MESH,
        ).wait_recv()

    def relay(k):
        to_x[k][0].wait_recv()
        on_y[k].start()
        to_y[k][1].wait_recv()
        on_x[k].start()

    def x_in(k):
        to_x[k][1].wait_recv()
        to_core[k][1].start()

    def y_in(k):
        to_y[k][0].wait_recv()
        to_core[k][2].start()

    def corner_in(k):
        on_x[k].wait_recv()
        on_y[k].wait_recv()
        to_core[k][3].start()

    def end_in(k):
        @pl.when(jnp.logical_not(middle))
        def _():
            z_on_wait(k)

    def sum_parts():
        for d in range(3):
            pltpu.make_async_remote_copy(
                src_ref=parts_in.at[0], dst_ref=parts_in.at[0], send_sem=send_sems.at[0],
                recv_sem=recv_sems.at[PART + (front + d + 1) % 4], device_id=core,
                device_id_type=pl.DeviceIdType.MESH,
            ).wait_recv()
        total = pivot[level] + parts_out[front]
        for d in range(3):
            total = total + parts_in[(front + d + 1) % 4]
        pivot[level] = total

    def before(i):
        if i == 0:
            own_in.wait()
            parent_in.wait()
        elif i == 1:
            relay(0)
            x_in(0)

            @pl.when(middle)
            def _():
                pass_on(1)
                pass_on(2)

            end_in(1)
            spread(1)
            y_in(0)
        elif i == 3:
            corner_in(0)
            for d in range(3):
                pltpu.make_async_remote_copy(
                    src_ref=codes, dst_ref=met.at[0], send_sem=send_sems.at[0],
                    recv_sem=recv_sems.at[META + (front + d + 1) % 4], device_id=core,
                    device_id_type=pl.DeviceIdType.MESH,
                ).wait_recv()

        elif i == 5:
            to_x[1][0].wait_recv()
            to_y[1][1].wait_recv()

            @pl.when(jnp.logical_not(middle) & (grid == 2))
            def _():
                on_y[1].start()

            @pl.when(jnp.logical_not(middle) & (grid == 1))
            def _():
                on_x[1].start()

            x_in(1)
            y_in(1)
        elif i == 7:
            relay(2)
        elif i == 8:
            end_in(3)
            spread(3)
            x_in(2)
            y_in(2)
        elif i == 10:
            corner_in(2)
        elif i == 12:

            @pl.when(is_first)
            def _():
                sum_parts()
                raw_x.start()
                raw_y.start()
        elif i == 14:
            corner_in(3)
            for g in (1, 2):

                @pl.when(grid == g)
                def _(g=g):
                    raw_x.wait_recv()
                    raw_on[g - 1].start()

    def between(i):
        if i == 4:

            @pl.when(middle)
            def _():
                pass_on(3)


            @pl.when(by_z)
            def _():
                zc_own.start()

            end_in(2)
            spread(2)

            @pl.when(is_first)
            def _():
                for copy in part_out:
                    copy.start()
        elif i == 11:

            @pl.when(to_z)
            def _():
                zc_wait(1)

            @pl.when(jnp.logical_not(to_z))
            def _():
                on_x[1].wait_recv()
                on_y[1].wait_recv()

            to_core[1][3].start()
        elif i == 12:
            relay(3)
            x_in(3)
            y_in(3)

    def expand(k, c):
        row = met[c, pl.ds(front, 1), :]
        ones = jnp.ones((row.shape[1], 128), jnp.bfloat16)
        ids = lax.broadcasted_iota(jnp.int32, (grids * spots * pieces, row.shape[1]), 0)
        hit = jnp.where(ids == row, 1.0, 0.0).astype(jnp.bfloat16)
        count = jnp.dot(hit, ones, preferred_element_type=jnp.float32)
        counts[k] = jnp.broadcast_to(
            count.reshape(grids, spots * pieces, 1, 128), (grids, spots * pieces, 8, 128)
        )

    def expand_parts():
        ids = lax.broadcasted_iota(jnp.int32, (grids * pieces, codes.shape[1]), 0)
        ids = (ids // pieces) * (spots * pieces) + ids % pieces
        ones = jnp.ones((codes.shape[1], 128), jnp.bfloat16)
        for q in range(ALL_FRONTS):
            hit = jnp.where(ids == codes[q : q + 1, :], 1.0, 0.0).astype(jnp.bfloat16)
            count = jnp.dot(hit, ones, preferred_element_type=jnp.float32)
            part_counts[q] = jnp.broadcast_to(
                count.reshape(grids * pieces, 1, 128), (grids * pieces, 8, 128)
            )

    def pick(ref, first, lane):
        value = ref[pl.ds(pl.multiple_of(first, ROWS), ROWS), lane : lane + half]
        return value.astype(jnp.float32).reshape(ROWS // 8, 8, half)

    def multiply(k, c, g):
        right = panels[c, g].reshape(levels * local * half, depth)
        left = panels[c, grid, level].reshape(local * half, depth)
        prod = lax.dot_general(left, right, NT, preferred_element_type=jnp.float32)
        tiles[...] = (-prod).astype(jnp.bfloat16)

        def add(i, carry):
            rows = pl.ds(pl.multiple_of(i * ROWS, ROWS), ROWS)
            parts = [
                [
                    pick(tiles, r * half + i * ROWS, (m * local + s) * half)
                    for r in range(local)
                    for s in range(local)
                ]
                for m in range(levels)
            ]
            for p in range(spots):
                lane = p % width_blocks * BLOCK
                many = [counts[k, g, p * pieces + x][None] for x in range(pieces)]
                for m in range(levels):
                    at = slice(lane + m * half, lane + (m + 1) * half)
                    total = acc[p // width_blocks, rows, at].reshape(ROWS // 8, 8, half)
                    for x in range(pieces):
                        total = total + many[x] * parts[m][x]
                    acc[p // width_blocks, rows, at] = total.reshape(ROWS, half)
            return carry

        lax.fori_loop(0, half // ROWS, add, 0)

    def add_parts(g):
        def add(i, carry):
            at_rows = pl.ds(pl.multiple_of(i * ROWS, ROWS), ROWS)
            for m in range(levels):
                at = slice(m * half, (m + 1) * half)
                piece = [
                    pick(tiles, r * half + i * ROWS, (m * local + s) * half)
                    for r in range(local)
                    for s in range(local)
                ]
                for q in range(ALL_FRONTS):
                    total = parts_out[q, at_rows, at].reshape(ROWS // 8, 8, half)
                    for x in range(pieces):
                        total = total + part_counts[q, g * pieces + x][None] * piece[x]
                    parts_out[q, at_rows, at] = total.reshape(ROWS, half)
            return carry

        lax.fori_loop(0, half // ROWS, add, 0)

    @pl.when(is_first)
    def _():
        raw_in.start()
        parts_out[...] = jnp.zeros_like(parts_out)
        expand_parts()
        raw_in.wait()

    def step(i, carry):
        for j in range(len(TURNS)):
            if j in BEFORE:

                @pl.when(i == j)
                def _(j=j):
                    before(j)

        k = choose(i, [t[0] for t in TURNS])
        p = choose(i, [t[1] for t in TURNS])
        c = choose(k, turn)
        g = choose(p, [grid, across, along, corner])
        pltpu.make_async_remote_copy(
            src_ref=panels.at[c, g, level], dst_ref=panels.at[c, g, level],
            send_sem=send_sems.at[0], recv_sem=recv_sems.at[CORE + 4 * k + p],
            device_id=core, device_id_type=pl.DeviceIdType.MESH,
        ).wait_recv()

        @pl.when(p == 0)
        def _():
            expand(k, c)

        multiply(k, c, g)

        @pl.when(is_first & (k == 0))
        def _():
            add_parts(g)

        for j in BETWEEN:

            @pl.when(i == j)
            def _(j=j):
                between(j)

        return carry

    lax.fori_loop(0, len(TURNS), step, 0)

    def whole():
        @pl.when(grid == 3)
        def _():
            raw_on[0].wait_recv()
            raw_on[1].wait_recv()

        pivot_core.start()
        pivot_core.wait_recv()
        return pivot[...].reshape(BLOCK, BLOCK)

    share_body(
        acc.at[:, :, pl.ds(0, BLOCK)], whole, shared, inverse, work,
        Sends(send_sems, recv_sems, used[0], SHARE), local_sems.at[4],
    )
    for when, copy in finish:
        if when is None:
            copy.wait_send()
        else:

            @pl.when(when)
            def _(copy=copy):
                copy.wait_send()


VMEM = pl.BlockSpec(memory_space=pltpu.VMEM)
HBM = pl.BlockSpec(memory_space=pltpu.HBM)
ANY = pl.BlockSpec(memory_space=pl.ANY)
SMEM = pl.BlockSpec(memory_space=pltpu.SMEM)


def owner_of(parents, parent_owner):
    ids = jnp.arange(parent_owner.shape[0], dtype=jnp.int32)
    return jnp.sum(jnp.where(parents[..., None] == ids, parent_owner, 0), axis=-1)


def assemble_all(
    child_panel, child_blocks, tile_rows, tile_cols, tile_parent, tile_place, parent_owner, parent_front
):
    levels, grids, fronts = lax.axis_size("lvl"), lax.axis_size("grid"), lax.axis_size("front")
    local, half, depth = child_panel.shape[1], child_panel.shape[4], child_panel.shape[5]
    parent_local, width = parent_front.shape[1], parent_front.shape[5]
    slots = tile_rows.shape[3]
    spots = parent_local * width // BLOCK
    pieces = local * local
    lanes = 2 * slots
    fields = [a.reshape(slots) for a in (tile_rows, tile_cols, tile_parent, tile_place)]
    fields += [parent_owner, child_blocks, jnp.zeros((lanes - fronts - 1,), jnp.int32)]
    fields = jnp.concatenate(fields).reshape(3, lanes)
    parent = parent_front.reshape(parent_local, half, width)
    sends = 100
    return pl.pallas_call(
        assemble_kernel,
        out_shape=(
            jax.ShapeDtypeStruct(parent.shape, jnp.float32),
            jax.ShapeDtypeStruct((grids, levels, parent_local, half, BLOCK), jnp.float32),
            jax.ShapeDtypeStruct((BLOCK, BLOCK), jnp.float32),
        ),
        in_specs=[ANY, VMEM, ANY],
        out_specs=(VMEM, VMEM, VMEM),
        scratch_shapes=[
            pltpu.VMEM((8, slots), jnp.int32),
            pltpu.VMEM((fronts, grids, levels, local, half, depth), jnp.bfloat16),
            pltpu.VMEM((fronts, 8, slots), jnp.int32),
            pltpu.VMEM((fronts, grids, spots * pieces, 8, 128), jnp.float32),
            pltpu.VMEM((fronts, grids * pieces, 8, 128), jnp.float32),
            pltpu.VMEM((local * half, levels * local * half), jnp.bfloat16),
            pltpu.VMEM((fronts, half, BLOCK), jnp.float32),
            pltpu.VMEM((fronts, half, BLOCK), jnp.float32),
            pltpu.VMEM((levels, half, BLOCK), jnp.float32),
            pltpu.VMEM((BLOCK, 2 * BLOCK), jnp.float32),
            pltpu.SemaphoreType.DMA((sends,)),
            pltpu.SemaphoreType.DMA((SHARE + 12,)),
            pltpu.SemaphoreType.DMA((9,)),
        ],
        compiler_params=pltpu.CompilerParams(
            collective_id=0, has_side_effects=True, vmem_limit_bytes=48 * 1024 * 1024
        ),
        name="assemble",
    )(
        child_panel.reshape(local, half, depth),
        fields,
        parent,
    )


def exchange_tiles(
    child_panel, child_blocks, tile_rows, tile_cols, tile_parent, tile_place, parent_owner, parent_front
):
    levels, grids, fronts = lax.axis_size("lvl"), lax.axis_size("grid"), lax.axis_size("front")
    grid_index = lax.axis_index("grid")
    local, half, depth = child_panel.shape[1], child_panel.shape[4], child_panel.shape[5]
    parent_local, width = parent_front.shape[1], parent_front.shape[5]
    slots = tile_rows.shape[3]
    blocks = width // BLOCK
    capacity = 2 * slots // fronts
    own = child_panel.reshape(local * half, depth)
    view = lax.all_gather(
        own.reshape(1, local, half, depth), ("grid", "lvl"), axis=0, tiled=True
    ).reshape(grids, levels, local, half, depth)
    gram = jnp.einsum("ik,glsjk->isglj", own, view, preferred_element_type=jnp.float32)
    gram = (-gram).astype(jnp.bfloat16).reshape(local, half, local * grids, BLOCK)
    gram = gram.transpose(0, 2, 1, 3).reshape(local * local * grids, half, BLOCK)
    row, col = tile_rows.reshape(slots), tile_cols.reshape(slots)
    live = (row * grids + grid_index < child_blocks[0]) & (col < child_blocks[0])
    owners = owner_of(tile_parent.reshape(slots), parent_owner)
    before = (jnp.arange(slots)[:, None] > jnp.arange(slots)[None, :]).astype(jnp.int32)
    same = (owners[:, None] == owners[None, :]).astype(jnp.int32)
    rank = jnp.sum(before * same, axis=1)
    index = owners * capacity + rank
    matches = index[None, :] == jnp.arange(fronts * capacity, dtype=jnp.int32)[:, None]
    filled = jnp.any(matches & live[None, :], axis=1)
    spans = local * grids
    pick = (row * spans + col)[:, None] == jnp.arange(local * spans, dtype=jnp.int32)[None, :]
    pick = jnp.any((matches & live[None, :])[:, :, None] & pick[None], axis=1)
    place = jnp.sum(jnp.where(matches, tile_place.reshape(slots)[None, :], 0), axis=1)
    outgoing = jnp.einsum(
        "kt,tij->kij", pick.astype(jnp.bfloat16), gram, preferred_element_type=jnp.float32
    ).astype(jnp.bfloat16)
    positions = jnp.where(filled, place, -1)
    incoming = lax.all_to_all(outgoing, "front", split_axis=0, concat_axis=0, tiled=True)
    landed = lax.all_to_all(positions, "front", split_axis=0, concat_axis=0, tiled=True)
    spots = parent_local * blocks
    selector = (landed[:, None] == jnp.arange(spots, dtype=jnp.int32)[None, :]).astype(jnp.bfloat16)
    contrib = jnp.einsum("sk,sij->kij", selector, incoming, preferred_element_type=jnp.float32)
    contrib = contrib.reshape(parent_local, blocks, half, BLOCK).transpose(0, 2, 1, 3)
    assembled = parent_front.reshape(parent_local, half, width) + contrib.reshape(
        parent_local, half, width
    )
    raw = lax.all_gather(assembled[0, :, :BLOCK][None], ("grid", "lvl"), axis=0, tiled=True)
    raw = raw[:levels].reshape(levels * half, BLOCK)
    return assembled, raw


def share_columns(assembled, pivot):
    levels, grids = lax.axis_size("lvl"), lax.axis_size("grid")
    column = assembled[:, :, :BLOCK]
    return pl.pallas_call(
        share_kernel,
        out_shape=(
            jax.ShapeDtypeStruct((grids, levels) + column.shape, jnp.float32),
            jax.ShapeDtypeStruct((BLOCK, BLOCK), jnp.float32),
        ),
        in_specs=[VMEM, VMEM],
        out_specs=(VMEM, VMEM),
        scratch_shapes=[
            pltpu.VMEM((BLOCK, 2 * BLOCK), jnp.float32),
            pltpu.SemaphoreType.DMA((12,)),
            pltpu.SemaphoreType.DMA((12,)),
            pltpu.SemaphoreType.DMA,
        ],
        compiler_params=pltpu.CompilerParams(
            collective_id=1, has_side_effects=True, vmem_limit_bytes=16 * 1024 * 1024
        ),
        name="share",
    )(column, pivot)


def per_device(*args):
    parent_front = args[-1]
    if lax.axis_size("front") == ALL_FRONTS:
        assembled, shared, inverse = assemble_all(*args)
    else:
        assembled, pivot = exchange_tiles(*args)
        shared, inverse = share_columns(assembled, pivot)
    local, half, width = assembled.shape
    result = pl.pallas_call(
        schur_kernel,
        out_shape=jax.ShapeDtypeStruct(assembled.shape, jnp.float32),
        in_specs=[VMEM, VMEM, VMEM],
        out_specs=ANY,
        scratch_shapes=[
            pltpu.VMEM((width // BLOCK, local, half, BLOCK), jnp.float32),
            pltpu.SemaphoreType.DMA((width // BLOCK,)),
        ],
        compiler_params=pltpu.CompilerParams(vmem_limit_bytes=20 * 1024 * 1024),
        name="schur",
    )(assembled, inverse, shared)
    return result.reshape(parent_front.shape)


def solution(mesh):
    return jax.shard_map(
        per_device,
        mesh=mesh,
        in_specs=(
            P("front", None, "grid", "lvl", None, None),
            P("front"),
            P("lvl", "front", "grid", None),
            P("lvl", "front", "grid", None),
            P("lvl", "front", "grid", None, None),
            P("lvl", "front", "grid", None),
            P(),
            P("front", None, "grid", "lvl", None, None),
        ),
        out_specs=P("front", None, "grid", "lvl", None, None),
        check_vma=False,
    )
```

```python
import functools

import jax
import jax.numpy as jnp
from jax import lax
from jax.experimental import pallas as pl
from jax.experimental.pallas import tpu as pltpu
from jax.sharding import PartitionSpec as P

BLOCK = 256
NB = 32
SUB = 8
HIGHEST = lax.Precision.HIGHEST
HIGH = lax.Precision.HIGH
NT = (((1,), (1,)), ((), ()))
TN = (((0,), (0,)), ((), ()))


def eliminate(work, inverse, begin, end):
    n, side = BLOCK, 128
    row_ids = lax.broadcasted_iota(jnp.int32, (NB, 1), 0)
    for kb in range(begin, end):
        first = kb * NB
        base = first // side * side
        low, high = base, base + 3 * side
        tiles = (high - low) // 128
        rows = work[first : first + NB, low:high]
        for sub in range(NB // SUB):
            at = first - low + sub * SUB
            cols = [
                jnp.broadcast_to(rows[:, at + i : at + i + 1], (NB, 128)) for i in range(SUB)
            ]
            for i in range(SUB):
                j = sub * SUB + i
                head = cols[i][j : j + 1, :]
                inv, per = lax.rsqrt(head), 1.0 / head
                for m in range(i + 1, SUB):
                    cols[m] = cols[m] - (cols[i] * cols[m][j : j + 1, :]) * per
                below = jnp.where(row_ids > j, cols[i] * inv, 0.0)
                urow = rows[j : j + 1, :] * jnp.concatenate([inv] * tiles, axis=1)
                wide = jnp.concatenate([below] * tiles, axis=1)
                rows = jnp.where(row_ids == j, urow, rows - wide * urow)
        if base == 0:
            inverse[first : first + NB, :side] = rows[:, n:high]
            inverse[first : first + NB, side:] = jnp.zeros((NB, n - side), jnp.float32)
        else:
            inverse[first : first + NB, :] = rows[:, n - low :]
        if first + NB < base + side:
            update = lax.dot_general(
                rows[:, :side], rows, TN, precision=HIGHEST, preferred_element_type=jnp.float32
            )
            work[first + NB : base + side, low:high] = (
                work[first + NB : base + side, low:high] - update[first + NB - base :, :]
            )
        if base == 0:
            work[first : first + NB, low:high] = rows
        if first + NB == side:
            update = lax.dot_general(
                work[:side, side:n],
                work[:side, side : n + side],
                TN,
                precision=HIGHEST,
                preferred_element_type=jnp.float32,
            )
            work[side:, side : n + side] = work[side:, side : n + side] - update


def schur_kernel(acc, inverse, shared, *rest):
    scales = rest[0] if len(rest) == 4 else None
    out, block, sems = rest[-3:]
    local, half, width = acc.shape
    grids, levels = shared.shape[0], shared.shape[1]
    blocks = width // BLOCK

    def put(b):
        lanes = pl.ds(pl.multiple_of(b * BLOCK, BLOCK), BLOCK)
        return pltpu.make_async_copy(block.at[b], out.at[:, :, lanes], sems.at[b])

    column = acc[:, :, :BLOCK].reshape(local * half, BLOCK)
    rows = lax.dot_general(
        column, inverse[...], NT, precision=HIGHEST, preferred_element_type=jnp.float32
    )
    block[0] = rows.reshape(local, half, BLOCK)
    put(0).start()
    weights = jnp.dot(rows, inverse[...], precision=HIGHEST, preferred_element_type=jnp.float32)
    for b in range(1, blocks):
        g, s = b % grids, b // grids
        other = shared[g, :, s].reshape(levels * half, BLOCK)
        if scales is not None:
            other = other.astype(jnp.int32).astype(jnp.float32)
        prod = lax.dot_general(
            weights, other, NT, precision=HIGH, preferred_element_type=jnp.float32
        )
        if scales is not None:
            row = [scales[g, lv, s, :1, :] for lv in range(levels)]
            prod = prod * jnp.concatenate(row, axis=1)
        prod = prod.reshape(local, half, BLOCK)
        block[b] = acc[:, :, b * BLOCK : (b + 1) * BLOCK] - prod
        put(b).start()
    for b in range(blocks):
        put(b).wait()


class Sends:
    def __init__(self, send_sems, recv_sems, first_send=0, first_recv=0):
        self.send_sems, self.recv_sems, self.started = send_sems, recv_sems, []
        self.first_send, self.first_recv, self.used = first_send, first_recv, 0

    def make(self, src, dst, device):
        copy = pltpu.make_async_remote_copy(
            src_ref=src,
            dst_ref=dst,
            send_sem=self.send_sems.at[self.first_send + self.used],
            recv_sem=self.recv_sems.at[self.first_recv + self.used],
            device_id=device,
            device_id_type=pl.DeviceIdType.MESH,
        )
        self.used += 1
        return copy

    def start(self, src, dst, device):
        copy = self.make(src, dst, device)
        copy.start()
        self.started.append(copy)
        return copy

    def finish(self):
        for copy in self.started:
            copy.wait_send()


def greet(devices):
    barrier = pltpu.get_barrier_semaphore()
    for device in devices:
        pl.semaphore_signal(barrier, inc=1, device_id=device, device_id_type=pl.DeviceIdType.MESH)
    pl.semaphore_wait(barrier, len(devices))


def plane_peers():
    level, grid = lax.axis_index("lvl"), lax.axis_index("grid")
    across = grid + 1 - 2 * (grid % 2)
    along = (grid + 2) % 4
    return level, grid, across, along


def share_kernel(own, pivot, out, inverse, work, send_sems, recv_sems, local_sem):
    level, grid, across, along = plane_peers()
    greet([{"grid": across}, {"grid": along}, {"lvl": 1 - level}])
    share_body(own, lambda: pivot[...], lambda: None, out, inverse, work, Sends(send_sems, recv_sems), local_sem)


def share_body(own, whole_pivot, meanwhile, out, inverse, work, sends, local_sem):
    level, grid, across, along = plane_peers()
    corner = (across + 2) % 4
    x_peer, y_peer, core = {"grid": across}, {"grid": along}, {"lvl": 1 - level}
    local = out.shape[2]
    mine = pltpu.make_async_copy(own, out.at[grid, level], local_sem)
    to_x = [None] * local
    to_y = [None] * local
    to_core = []
    for r in range(local):
        place = out.at[grid, level, r]
        to_x[r] = sends.start(own.at[r], place, x_peer)
        place = out.at[grid, level, local - 1 - r]
        to_y[local - 1 - r] = sends.start(own.at[local - 1 - r], place, y_peer)
    to_core.append(sends.start(own, out.at[grid, level], core))
    mine.start()
    whole = whole_pivot()
    work[:, :BLOCK] = 0.5 * (whole + whole.T)
    work[:, BLOCK:] = (
        lax.broadcasted_iota(jnp.int32, (BLOCK, BLOCK), 0)
        == lax.broadcasted_iota(jnp.int32, (BLOCK, BLOCK), 1)
    ).astype(jnp.float32)
    eliminate(work, inverse, 0, 4)
    meanwhile()
    to_x[0].wait_recv()
    half = out.at[across, level, 0]
    corner_y = sends.start(half, half, y_peer)
    to_y[1].wait_recv()
    half = out.at[along, level, 1]
    corner_x = sends.start(half, half, x_peer)
    for r in range(1, local):
        to_x[r].wait_recv()
    place = out.at[across, level]
    to_core.append(sends.start(place, place, core))
    to_y[0].wait_recv()
    place = out.at[along, level]
    to_core.append(sends.start(place, place, core))
    eliminate(work, inverse, 4, BLOCK // NB)
    corner_y.wait_recv()
    half = out.at[corner, level, 0]
    to_core.append(sends.start(half, half, core))
    corner_x.wait_recv()
    half = out.at[corner, level, 1]
    to_core.append(sends.start(half, half, core))
    mine.wait()
    for copy in to_core:
        copy.wait_recv()
    sends.finish()


ALL_FRONTS = 4
TURNS = (
    (0, 0), (0, 1), (0, 2), (1, 0), (0, 3), (2, 0), (1, 1), (1, 2),
    (3, 0), (2, 1), (2, 2), (2, 3), (1, 3), (3, 1), (3, 2), (3, 3),
)
BEFORE = (0, 1, 3, 5, 7, 8, 10, 12, 14)
BETWEEN = (4, 11, 12)
ROWS = 16
Z, ZC, XH, YH, CX, CY, CORE, META, PART, RAW = 0, 4, 8, 16, 24, 28, 32, 48, 52, 56
SCALE = 60
SHARE = 68
STEPS = 32767.0


def choose(index, values):
    out = jnp.int32(values[0])
    for i in range(1, len(values)):
        out = jnp.where(index == i, values[i], out)
    return out


def assemble_kernel(
    own, fields, parent,
    acc, shared, scales, inverse,
    codes, panels, met, counts, part_counts, tiles, parts_out, parts_in, pivot, work, column,
    send_sems, recv_sems, local_sems,
):
    level, grid, across, along = plane_peers()
    corner = (across + 2) % 4
    front = lax.axis_index("front")
    pair, inner = front + 1 - 2 * (front % 2), 3 - front
    turn = [front, pair, 2 - front // 2, 3 - 3 * (front // 2)]
    middle = (front == 1) | (front == 2)
    local, half, depth = own.shape
    levels, grids = panels.shape[2], panels.shape[1]
    spots = acc.shape[0] * acc.shape[2] // BLOCK
    width_blocks = acc.shape[2] // BLOCK
    pieces = local * local
    x_peer, y_peer, core = {"grid": across}, {"grid": along}, {"lvl": 1 - level}
    fronts = [{"front": pair}, {"front": (front + 2) % 4}, {"front": inner}]
    plane = [x_peer, y_peer, {"grid": corner}, core] + [
        {"grid": g, "lvl": 1 - level} for g in (across, along, corner)
    ]

    used = [0]
    finish = []

    def remote(src, dst, recv, device, when=None):
        copy = pltpu.make_async_remote_copy(
            src_ref=src,
            dst_ref=dst,
            send_sem=send_sems.at[used[0]],
            recv_sem=recv_sems.at[recv],
            device_id=device,
            device_id_type=pl.DeviceIdType.MESH,
        )
        used[0] += 1
        finish.append((when, copy))
        return copy

    def at(k, g, lv=level):
        return panels.at[turn[k], g, lv]

    parent_in = pltpu.make_async_copy(parent, acc, local_sems.at[0])
    own_in = pltpu.make_async_copy(own, at(0, grid), local_sems.at[1])
    for copy in [own_in, parent_in]:
        copy.start()

    met_out = [remote(codes, met.at[front], META + front, d) for d in fronts]
    z_own = remote(own, at(0, grid), Z + front, {"front": pair})
    z_own_in = remote(own, at(0, grid), Z + front, {"front": inner}, middle)
    z_on = [None] + [
        remote(at(k, grid), at(k, grid), Z + turn[k], {"front": to}, middle)
        for k, to in ((1, inner), (2, pair), (3, pair))
    ]
    by_z = jnp.logical_not(middle & (grid == 0))
    to_z = jnp.logical_not(jnp.logical_not(middle) & (grid == 0))
    zc_own = remote(at(0, corner), at(0, corner), ZC + front, {"front": pair}, by_z)
    to_x, to_y, to_core, on_x, on_y = [], [], [], {}, {}
    for k in range(4):
        mine = own if k == 0 else at(k, grid)
        to_x.append([remote(mine.at[h], at(k, grid).at[h], XH + 2 * k + h, x_peer) for h in (0, 1)])
        to_y.append([remote(mine.at[h], at(k, grid).at[h], YH + 2 * k + h, y_peer) for h in (0, 1)])
        sources = [mine, at(k, across), at(k, along), at(k, corner)]
        to_core.append([
            remote(source, at(k, g), CORE + 4 * k + p, core)
            for p, (source, g) in enumerate(zip(sources, (grid, across, along, corner)))
        ])
        x_half, y_half = at(k, across).at[0], at(k, along).at[1]
        by_y, by_x = None, None
        if k == 1:
            by_y = jnp.logical_not(middle) & (grid == 2)
            by_x = jnp.logical_not(middle) & (grid == 1)
        on_y[k] = remote(x_half, x_half, CY + k, y_peer, by_y)
        on_x[k] = remote(y_half, y_half, CX + k, x_peer, by_x)
    is_first = grid == 0
    part_out = [
        remote(parts_out.at[q], parts_in.at[front], PART + front, d, is_first)
        for q, d in zip((pair, (front + 2) % 4, inner), fronts)
    ]
    rows = pivot.at[level]
    raw_x = remote(rows, rows, RAW, x_peer, is_first)
    raw_y = remote(rows, rows, RAW, y_peer, is_first)
    raw_in = pltpu.make_async_copy(parent.at[0, :, pl.ds(0, BLOCK)], rows, local_sems.at[3])
    raw_halves = [pivot.at[level, pl.ds(h * (half // 2), half // 2)] for h in (0, 1)]
    raw_on = [
        remote(raw_halves[0], raw_halves[0], RAW + 1, y_peer, grid == 1),
        remote(raw_halves[1], raw_halves[1], RAW + 2, x_peer, grid == 2),
    ]
    scale_at = scales.at[grid, level]
    scale_out = [remote(scale_at, scale_at, SCALE + 2 * grid + level, d) for d in plane]
    pivot_core = remote(rows, rows, RAW + 3, core)

    slots = codes.shape[1]
    row, col, named, spot = [
        fields[i : i + 1, j * slots : (j + 1) * slots] for i in (0, 1) for j in (0, 1)
    ]
    blocks = fields[2:3, ALL_FRONTS : ALL_FRONTS + 1]
    live = (row * grids + grid < blocks) & (col < blocks)
    owner = jnp.zeros_like(named)
    for q in range(ALL_FRONTS):
        owner = jnp.where(named == q, fields[2:3, q : q + 1], owner)
    code = (col % grids) * (spots * pieces) + spot * pieces + row * local + col // grids
    code = jnp.where(live, code, -1)
    ids = lax.broadcasted_iota(jnp.int32, codes.shape, 0)
    codes[...] = jnp.where(owner == ids, code, -1)
    met[pl.ds(front, 1)] = codes[...][None]
    greet(fronts + plane)

    def spread(k):
        to_x[k][0].start()
        to_y[k][1].start()
        to_core[k][0].start()
        to_x[k][1].start()
        to_y[k][0].start()

    z_own.start()

    @pl.when(middle)
    def _():
        z_own_in.start()

    for copy in met_out:
        copy.start()
    spread(0)

    def pass_on(k):
        z_on_wait(k)
        z_on[k].start()

    def z_on_wait(k):
        pltpu.make_async_remote_copy(
            src_ref=at(k, grid), dst_ref=at(k, grid), send_sem=send_sems.at[0],
            recv_sem=recv_sems.at[Z + turn[k]], device_id=core, device_id_type=pl.DeviceIdType.MESH,
        ).wait_recv()

    def zc_wait(k):
        pltpu.make_async_remote_copy(
            src_ref=at(k, corner), dst_ref=at(k, corner), send_sem=send_sems.at[0],
            recv_sem=recv_sems.at[ZC + turn[k]], device_id=core, device_id_type=pl.DeviceIdType.MESH,
        ).wait_recv()

    def relay(k):
        to_x[k][0].wait_recv()
        on_y[k].start()
        to_y[k][1].wait_recv()
        on_x[k].start()

    def x_in(k):
        to_x[k][1].wait_recv()
        to_core[k][1].start()

    def y_in(k):
        to_y[k][0].wait_recv()
        to_core[k][2].start()

    def corner_in(k):
        on_x[k].wait_recv()
        on_y[k].wait_recv()
        to_core[k][3].start()

    def end_in(k):
        @pl.when(jnp.logical_not(middle))
        def _():
            z_on_wait(k)

    def sum_parts():
        for d in range(3):
            pltpu.make_async_remote_copy(
                src_ref=parts_in.at[0], dst_ref=parts_in.at[0], send_sem=send_sems.at[0],
                recv_sem=recv_sems.at[PART + (front + d + 1) % 4], device_id=core,
                device_id_type=pl.DeviceIdType.MESH,
            ).wait_recv()
        total = pivot[level] + parts_out[front]
        for d in range(3):
            total = total + parts_in[(front + d + 1) % 4]
        pivot[level] = total

    def before(i):
        if i == 0:
            own_in.wait()
            parent_in.wait()
        elif i == 1:
            relay(0)
            x_in(0)

            @pl.when(middle)
            def _():
                pass_on(1)
                pass_on(2)

            end_in(1)
            spread(1)
            y_in(0)
        elif i == 3:
            corner_in(0)
            for d in range(3):
                pltpu.make_async_remote_copy(
                    src_ref=codes, dst_ref=met.at[0], send_sem=send_sems.at[0],
                    recv_sem=recv_sems.at[META + (front + d + 1) % 4], device_id=core,
                    device_id_type=pl.DeviceIdType.MESH,
                ).wait_recv()

        elif i == 5:
            to_x[1][0].wait_recv()
            to_y[1][1].wait_recv()

            @pl.when(jnp.logical_not(middle) & (grid == 2))
            def _():
                on_y[1].start()

            @pl.when(jnp.logical_not(middle) & (grid == 1))
            def _():
                on_x[1].start()

            x_in(1)
            y_in(1)
        elif i == 7:
            relay(2)
        elif i == 8:
            end_in(3)
            spread(3)
            x_in(2)
            y_in(2)
        elif i == 10:
            corner_in(2)
        elif i == 12:

            @pl.when(is_first)
            def _():
                sum_parts()
                raw_x.start()
                raw_y.start()
        elif i == 14:
            corner_in(3)
            for g in (1, 2):

                @pl.when(grid == g)
                def _(g=g):
                    raw_x.wait_recv()
                    raw_on[g - 1].start()

    def between(i):
        if i == 4:

            @pl.when(middle)
            def _():
                pass_on(3)


            @pl.when(by_z)
            def _():
                zc_own.start()

            end_in(2)
            spread(2)

            @pl.when(is_first)
            def _():
                for copy in part_out:
                    copy.start()
        elif i == 11:

            @pl.when(to_z)
            def _():
                zc_wait(1)

            @pl.when(jnp.logical_not(to_z))
            def _():
                on_x[1].wait_recv()
                on_y[1].wait_recv()

            to_core[1][3].start()
        elif i == 12:
            relay(3)
            x_in(3)
            y_in(3)

    def expand(k, c):
        row = met[c, pl.ds(front, 1), :]
        ones = jnp.ones((row.shape[1], 128), jnp.bfloat16)
        ids = lax.broadcasted_iota(jnp.int32, (grids * spots * pieces, row.shape[1]), 0)
        hit = jnp.where(ids == row, 1.0, 0.0).astype(jnp.bfloat16)
        count = jnp.dot(hit, ones, preferred_element_type=jnp.float32)
        counts[k] = jnp.broadcast_to(
            count.reshape(grids, spots * pieces, 1, 128), (grids, spots * pieces, 8, 128)
        )

    def expand_parts():
        ids = lax.broadcasted_iota(jnp.int32, (grids * pieces, codes.shape[1]), 0)
        ids = (ids // pieces) * (spots * pieces) + ids % pieces
        ones = jnp.ones((codes.shape[1], 128), jnp.bfloat16)
        for q in range(ALL_FRONTS):
            hit = jnp.where(ids == codes[q : q + 1, :], 1.0, 0.0).astype(jnp.bfloat16)
            count = jnp.dot(hit, ones, preferred_element_type=jnp.float32)
            part_counts[q] = jnp.broadcast_to(
                count.reshape(grids * pieces, 1, 128), (grids * pieces, 8, 128)
            )

    def pick(ref, first, lane):
        value = ref[pl.ds(pl.multiple_of(first, ROWS), ROWS), lane : lane + half]
        return value.astype(jnp.float32).reshape(ROWS // 8, 8, half)

    def multiply(k, c, g):
        right = panels[c, g].reshape(levels * local * half, depth)
        left = panels[c, grid, level].reshape(local * half, depth)
        prod = lax.dot_general(left, right, NT, preferred_element_type=jnp.float32)
        tiles[...] = (-prod).astype(jnp.bfloat16)

        def add(i, carry):
            rows = pl.ds(pl.multiple_of(i * ROWS, ROWS), ROWS)
            parts = [
                [
                    pick(tiles, r * half + i * ROWS, (m * local + s) * half)
                    for r in range(local)
                    for s in range(local)
                ]
                for m in range(levels)
            ]
            for p in range(spots):
                lane = p % width_blocks * BLOCK
                many = [counts[k, g, p * pieces + x][None] for x in range(pieces)]
                for m in range(levels):
                    at = slice(lane + m * half, lane + (m + 1) * half)
                    total = acc[p // width_blocks, rows, at].reshape(ROWS // 8, 8, half)
                    for x in range(pieces):
                        total = total + many[x] * parts[m][x]
                    acc[p // width_blocks, rows, at] = total.reshape(ROWS, half)
            return carry

        lax.fori_loop(0, half // ROWS, add, 0)

    def add_parts(g):
        def add(i, carry):
            at_rows = pl.ds(pl.multiple_of(i * ROWS, ROWS), ROWS)
            for m in range(levels):
                at = slice(m * half, (m + 1) * half)
                piece = [
                    pick(tiles, r * half + i * ROWS, (m * local + s) * half)
                    for r in range(local)
                    for s in range(local)
                ]
                for q in range(ALL_FRONTS):
                    total = parts_out[q, at_rows, at].reshape(ROWS // 8, 8, half)
                    for x in range(pieces):
                        total = total + part_counts[q, g * pieces + x][None] * piece[x]
                    parts_out[q, at_rows, at] = total.reshape(ROWS, half)
            return carry

        lax.fori_loop(0, half // ROWS, add, 0)

    @pl.when(is_first)
    def _():
        raw_in.start()
        parts_out[...] = jnp.zeros_like(parts_out)
        expand_parts()
        raw_in.wait()

    def step(i, carry):
        for j in range(len(TURNS)):
            if j in BEFORE:

                @pl.when(i == j)
                def _(j=j):
                    before(j)

        k = choose(i, [t[0] for t in TURNS])
        p = choose(i, [t[1] for t in TURNS])
        c = choose(k, turn)
        g = choose(p, [grid, across, along, corner])
        pltpu.make_async_remote_copy(
            src_ref=panels.at[c, g, level], dst_ref=panels.at[c, g, level],
            send_sem=send_sems.at[0], recv_sem=recv_sems.at[CORE + 4 * k + p],
            device_id=core, device_id_type=pl.DeviceIdType.MESH,
        ).wait_recv()

        @pl.when(p == 0)
        def _():
            expand(k, c)

        multiply(k, c, g)

        @pl.when(is_first & (k == 0))
        def _():
            add_parts(g)

        for j in BETWEEN:

            @pl.when(i == j)
            def _(j=j):
                between(j)

        return carry

    lax.fori_loop(0, len(TURNS), step, 0)

    @pl.when(grid == 3)
    def _():
        raw_on[0].wait_recv()
        raw_on[1].wait_recv()

    pivot_core.start()
    peaks = []
    for r in range(local):
        value = acc[r, :, :BLOCK]
        largest = jnp.maximum(jnp.max(jnp.abs(value), axis=1, keepdims=True), 1e-30)
        value = value * (STEPS / largest)
        value = value + jnp.where(value < 0.0, -0.5, 0.5)
        column[r] = value.astype(jnp.int32).astype(jnp.int16)
        peaks.append(largest)

    def whole():
        pivot_core.wait_recv()
        return pivot[...].reshape(BLOCK, BLOCK)

    def send_scales():
        for r in range(local):
            wide = jnp.broadcast_to(peaks[r] * (1.0 / STEPS), (half, half))
            scales[grid, level, r] = wide.T[:8, :]
        for copy in scale_out:
            copy.start()

    share_body(
        column, whole, send_scales, shared, inverse, work,
        Sends(send_sems, recv_sems, used[0], SHARE), local_sems.at[4],
    )
    for g in (across, along, corner, grid):
        for lv in (level, 1 - level):
            if g is grid and lv is level:
                continue
            pltpu.make_async_remote_copy(
                src_ref=scale_at, dst_ref=scales.at[g, lv], send_sem=send_sems.at[0],
                recv_sem=recv_sems.at[SCALE + 2 * g + lv], device_id=core,
                device_id_type=pl.DeviceIdType.MESH,
            ).wait_recv()
    for when, copy in finish:
        if when is None:
            copy.wait_send()
        else:

            @pl.when(when)
            def _(copy=copy):
                copy.wait_send()


VMEM = pl.BlockSpec(memory_space=pltpu.VMEM)
HBM = pl.BlockSpec(memory_space=pltpu.HBM)
ANY = pl.BlockSpec(memory_space=pl.ANY)
SMEM = pl.BlockSpec(memory_space=pltpu.SMEM)


def owner_of(parents, parent_owner):
    ids = jnp.arange(parent_owner.shape[0], dtype=jnp.int32)
    return jnp.sum(jnp.where(parents[..., None] == ids, parent_owner, 0), axis=-1)


def assemble_all(
    child_panel, child_blocks, tile_rows, tile_cols, tile_parent, tile_place, parent_owner, parent_front
):
    levels, grids, fronts = lax.axis_size("lvl"), lax.axis_size("grid"), lax.axis_size("front")
    local, half, depth = child_panel.shape[1], child_panel.shape[4], child_panel.shape[5]
    parent_local, width = parent_front.shape[1], parent_front.shape[5]
    slots = tile_rows.shape[3]
    spots = parent_local * width // BLOCK
    pieces = local * local
    lanes = 2 * slots
    fields = [a.reshape(slots) for a in (tile_rows, tile_cols, tile_parent, tile_place)]
    fields += [parent_owner, child_blocks, jnp.zeros((lanes - fronts - 1,), jnp.int32)]
    fields = jnp.concatenate(fields).reshape(3, lanes)
    parent = parent_front.reshape(parent_local, half, width)
    sends = 110
    return pl.pallas_call(
        assemble_kernel,
        out_shape=(
            jax.ShapeDtypeStruct(parent.shape, jnp.float32),
            jax.ShapeDtypeStruct((grids, levels, parent_local, half, BLOCK), jnp.int16),
            jax.ShapeDtypeStruct((grids, levels, parent_local, 8, half), jnp.float32),
            jax.ShapeDtypeStruct((BLOCK, BLOCK), jnp.float32),
        ),
        in_specs=[ANY, VMEM, ANY],
        out_specs=(VMEM,) * 4,
        scratch_shapes=[
            pltpu.VMEM((8, slots), jnp.int32),
            pltpu.VMEM((fronts, grids, levels, local, half, depth), jnp.bfloat16),
            pltpu.VMEM((fronts, 8, slots), jnp.int32),
            pltpu.VMEM((fronts, grids, spots * pieces, 8, 128), jnp.float32),
            pltpu.VMEM((fronts, grids * pieces, 8, 128), jnp.float32),
            pltpu.VMEM((local * half, levels * local * half), jnp.bfloat16),
            pltpu.VMEM((fronts, half, BLOCK), jnp.float32),
            pltpu.VMEM((fronts, half, BLOCK), jnp.float32),
            pltpu.VMEM((levels, half, BLOCK), jnp.float32),
            pltpu.VMEM((BLOCK, 2 * BLOCK), jnp.float32),
            pltpu.VMEM((parent_local, half, BLOCK), jnp.int16),
            pltpu.SemaphoreType.DMA((sends,)),
            pltpu.SemaphoreType.DMA((SHARE + 12,)),
            pltpu.SemaphoreType.DMA((9,)),
        ],
        compiler_params=pltpu.CompilerParams(
            collective_id=0, has_side_effects=True, vmem_limit_bytes=50 * 1024 * 1024
        ),
        name="assemble",
    )(
        child_panel.reshape(local, half, depth),
        fields,
        parent,
    )


def exchange_tiles(
    child_panel, child_blocks, tile_rows, tile_cols, tile_parent, tile_place, parent_owner, parent_front
):
    levels, grids, fronts = lax.axis_size("lvl"), lax.axis_size("grid"), lax.axis_size("front")
    grid_index = lax.axis_index("grid")
    local, half, depth = child_panel.shape[1], child_panel.shape[4], child_panel.shape[5]
    parent_local, width = parent_front.shape[1], parent_front.shape[5]
    slots = tile_rows.shape[3]
    blocks = width // BLOCK
    capacity = 2 * slots // fronts
    own = child_panel.reshape(local * half, depth)
    view = lax.all_gather(
        own.reshape(1, local, half, depth), ("grid", "lvl"), axis=0, tiled=True
    ).reshape(grids, levels, local, half, depth)
    gram = jnp.einsum("ik,glsjk->isglj", own, view, preferred_element_type=jnp.float32)
    gram = (-gram).astype(jnp.bfloat16).reshape(local, half, local * grids, BLOCK)
    gram = gram.transpose(0, 2, 1, 3).reshape(local * local * grids, half, BLOCK)
    row, col = tile_rows.reshape(slots), tile_cols.reshape(slots)
    live = (row * grids + grid_index < child_blocks[0]) & (col < child_blocks[0])
    owners = owner_of(tile_parent.reshape(slots), parent_owner)
    before = (jnp.arange(slots)[:, None] > jnp.arange(slots)[None, :]).astype(jnp.int32)
    same = (owners[:, None] == owners[None, :]).astype(jnp.int32)
    rank = jnp.sum(before * same, axis=1)
    index = owners * capacity + rank
    matches = index[None, :] == jnp.arange(fronts * capacity, dtype=jnp.int32)[:, None]
    filled = jnp.any(matches & live[None, :], axis=1)
    spans = local * grids
    pick = (row * spans + col)[:, None] == jnp.arange(local * spans, dtype=jnp.int32)[None, :]
    pick = jnp.any((matches & live[None, :])[:, :, None] & pick[None], axis=1)
    place = jnp.sum(jnp.where(matches, tile_place.reshape(slots)[None, :], 0), axis=1)
    outgoing = jnp.einsum(
        "kt,tij->kij", pick.astype(jnp.bfloat16), gram, preferred_element_type=jnp.float32
    ).astype(jnp.bfloat16)
    positions = jnp.where(filled, place, -1)
    incoming = lax.all_to_all(outgoing, "front", split_axis=0, concat_axis=0, tiled=True)
    landed = lax.all_to_all(positions, "front", split_axis=0, concat_axis=0, tiled=True)
    spots = parent_local * blocks
    selector = (landed[:, None] == jnp.arange(spots, dtype=jnp.int32)[None, :]).astype(jnp.bfloat16)
    contrib = jnp.einsum("sk,sij->kij", selector, incoming, preferred_element_type=jnp.float32)
    contrib = contrib.reshape(parent_local, blocks, half, BLOCK).transpose(0, 2, 1, 3)
    assembled = parent_front.reshape(parent_local, half, width) + contrib.reshape(
        parent_local, half, width
    )
    raw = lax.all_gather(assembled[0, :, :BLOCK][None], ("grid", "lvl"), axis=0, tiled=True)
    raw = raw[:levels].reshape(levels * half, BLOCK)
    return assembled, raw


def share_columns(assembled, pivot):
    levels, grids = lax.axis_size("lvl"), lax.axis_size("grid")
    column = assembled[:, :, :BLOCK]
    return pl.pallas_call(
        share_kernel,
        out_shape=(
            jax.ShapeDtypeStruct((grids, levels) + column.shape, jnp.float32),
            jax.ShapeDtypeStruct((BLOCK, BLOCK), jnp.float32),
        ),
        in_specs=[VMEM, VMEM],
        out_specs=(VMEM, VMEM),
        scratch_shapes=[
            pltpu.VMEM((BLOCK, 2 * BLOCK), jnp.float32),
            pltpu.SemaphoreType.DMA((12,)),
            pltpu.SemaphoreType.DMA((12,)),
            pltpu.SemaphoreType.DMA,
        ],
        compiler_params=pltpu.CompilerParams(
            collective_id=1, has_side_effects=True, vmem_limit_bytes=16 * 1024 * 1024
        ),
        name="share",
    )(column, pivot)


def per_device(*args):
    parent_front = args[-1]
    if lax.axis_size("front") == ALL_FRONTS:
        assembled, *column, inverse = assemble_all(*args)
    else:
        assembled, pivot = exchange_tiles(*args)
        shared, inverse = share_columns(assembled, pivot)
        column = [shared]
    local, half, width = assembled.shape
    result = pl.pallas_call(
        schur_kernel,
        out_shape=jax.ShapeDtypeStruct(assembled.shape, jnp.float32),
        in_specs=[VMEM] * (2 + len(column)),
        out_specs=ANY,
        scratch_shapes=[
            pltpu.VMEM((width // BLOCK, local, half, BLOCK), jnp.float32),
            pltpu.SemaphoreType.DMA((width // BLOCK,)),
        ],
        compiler_params=pltpu.CompilerParams(vmem_limit_bytes=20 * 1024 * 1024),
        name="schur",
    )(assembled, inverse, *column)
    return result.reshape(parent_front.shape)


def solution(mesh):
    return jax.shard_map(
        per_device,
        mesh=mesh,
        in_specs=(
            P("front", None, "grid", "lvl", None, None),
            P("front"),
            P("lvl", "front", "grid", None),
            P("lvl", "front", "grid", None),
            P("lvl", "front", "grid", None, None),
            P("lvl", "front", "grid", None),
            P(),
            P("front", None, "grid", "lvl", None, None),
        ),
        out_specs=P("front", None, "grid", "lvl", None, None),
        check_vma=False,
    )
```

```python
import functools

import jax
import jax.numpy as jnp
from jax import lax
from jax.experimental import pallas as pl
from jax.experimental.pallas import tpu as pltpu
from jax.sharding import PartitionSpec as P

BLOCK = 256
NB = 32
SUB = 8
HIGHEST = lax.Precision.HIGHEST
HIGH = lax.Precision.HIGH
NT = (((1,), (1,)), ((), ()))
TN = (((0,), (0,)), ((), ()))


def eliminate(work, inverse, begin, end):
    n, side = BLOCK, 128
    row_ids = lax.broadcasted_iota(jnp.int32, (NB, 1), 0)
    for kb in range(begin, end):
        first = kb * NB
        base = first // side * side
        low, high = base, base + 3 * side
        tiles = (high - low) // 128
        rows = work[first : first + NB, low:high]
        for sub in range(NB // SUB):
            at = first - low + sub * SUB
            cols = [
                jnp.broadcast_to(rows[:, at + i : at + i + 1], (NB, 128)) for i in range(SUB)
            ]
            for i in range(SUB):
                j = sub * SUB + i
                head = cols[i][j : j + 1, :]
                inv, per = lax.rsqrt(head), 1.0 / head
                for m in range(i + 1, SUB):
                    cols[m] = cols[m] - (cols[i] * cols[m][j : j + 1, :]) * per
                below = jnp.where(row_ids > j, cols[i] * inv, 0.0)
                urow = rows[j : j + 1, :] * jnp.concatenate([inv] * tiles, axis=1)
                wide = jnp.concatenate([below] * tiles, axis=1)
                rows = jnp.where(row_ids == j, urow, rows - wide * urow)
        if base == 0:
            inverse[first : first + NB, :side] = rows[:, n:high]
            inverse[first : first + NB, side:] = jnp.zeros((NB, n - side), jnp.float32)
        else:
            inverse[first : first + NB, :] = rows[:, n - low :]
        if first + NB < base + side:
            update = lax.dot_general(
                rows[:, :side], rows, TN, precision=HIGHEST, preferred_element_type=jnp.float32
            )
            work[first + NB : base + side, low:high] = (
                work[first + NB : base + side, low:high] - update[first + NB - base :, :]
            )
        if base == 0:
            work[first : first + NB, low:high] = rows
        if first + NB == side:
            update = lax.dot_general(
                work[:side, side:n],
                work[:side, side : n + side],
                TN,
                precision=HIGHEST,
                preferred_element_type=jnp.float32,
            )
            work[side:, side : n + side] = work[side:, side : n + side] - update


def schur_kernel(acc, inverse, shared, *rest):
    scales = rest[0] if len(rest) == 4 else None
    out, block, sems = rest[-3:]
    local, half, width = acc.shape
    grids, levels = shared.shape[0], shared.shape[1]
    blocks = width // BLOCK

    def put(b):
        lanes = pl.ds(pl.multiple_of(b * BLOCK, BLOCK), BLOCK)
        return pltpu.make_async_copy(block.at[b], out.at[:, :, lanes], sems.at[b])

    column = acc[:, :, :BLOCK].reshape(local * half, BLOCK)
    rows = lax.dot_general(
        column, inverse[...], NT, precision=HIGHEST, preferred_element_type=jnp.float32
    )
    block[0] = rows.reshape(local, half, BLOCK)
    put(0).start()
    weights = jnp.dot(rows, inverse[...], precision=HIGHEST, preferred_element_type=jnp.float32)
    for b in range(1, blocks):
        g, s = b % grids, b // grids
        other = shared[g, :, s].reshape(levels * half, BLOCK)
        if scales is not None:
            other = other.astype(jnp.int32).astype(jnp.float32)
        prod = lax.dot_general(
            weights, other, NT, precision=HIGH, preferred_element_type=jnp.float32
        )
        if scales is not None:
            row = [scales[g, lv, s, :1, :] for lv in range(levels)]
            prod = prod * jnp.concatenate(row, axis=1)
        prod = prod.reshape(local, half, BLOCK)
        block[b] = acc[:, :, b * BLOCK : (b + 1) * BLOCK] - prod
        put(b).start()
    for b in range(blocks):
        put(b).wait()


class Sends:
    def __init__(self, send_sems, recv_sems, first_send=0, first_recv=0):
        self.send_sems, self.recv_sems, self.started = send_sems, recv_sems, []
        self.first_send, self.first_recv, self.used = first_send, first_recv, 0

    def make(self, src, dst, device):
        copy = pltpu.make_async_remote_copy(
            src_ref=src,
            dst_ref=dst,
            send_sem=self.send_sems.at[self.first_send + self.used],
            recv_sem=self.recv_sems.at[self.first_recv + self.used],
            device_id=device,
            device_id_type=pl.DeviceIdType.MESH,
        )
        self.used += 1
        return copy

    def start(self, src, dst, device):
        copy = self.make(src, dst, device)
        copy.start()
        self.started.append(copy)
        return copy

    def finish(self):
        for copy in self.started:
            copy.wait_send()


def greet(devices):
    barrier = pltpu.get_barrier_semaphore()
    for device in devices:
        pl.semaphore_signal(barrier, inc=1, device_id=device, device_id_type=pl.DeviceIdType.MESH)
    pl.semaphore_wait(barrier, len(devices))


def plane_peers():
    level, grid = lax.axis_index("lvl"), lax.axis_index("grid")
    across = grid + 1 - 2 * (grid % 2)
    along = (grid + 2) % 4
    return level, grid, across, along


def share_kernel(own, pivot, out, inverse, work, send_sems, recv_sems, local_sem):
    level, grid, across, along = plane_peers()
    greet([{"grid": across}, {"grid": along}, {"lvl": 1 - level}])
    share_body(own, lambda: pivot[...], lambda: None, out, inverse, work, Sends(send_sems, recv_sems), local_sem)


def share_body(own, whole_pivot, meanwhile, out, inverse, work, sends, local_sem):
    level, grid, across, along = plane_peers()
    corner = (across + 2) % 4
    x_peer, y_peer, core = {"grid": across}, {"grid": along}, {"lvl": 1 - level}
    local = out.shape[2]
    mine = pltpu.make_async_copy(own, out.at[grid, level], local_sem)
    to_x = [None] * local
    to_y = [None] * local
    to_core = []
    for r in range(local):
        place = out.at[grid, level, r]
        to_x[r] = sends.start(own.at[r], place, x_peer)
        place = out.at[grid, level, local - 1 - r]
        to_y[local - 1 - r] = sends.start(own.at[local - 1 - r], place, y_peer)
    to_core.append(sends.start(own, out.at[grid, level], core))
    mine.start()
    whole = whole_pivot()
    work[:, :BLOCK] = 0.5 * (whole + whole.T)
    work[:, BLOCK:] = (
        lax.broadcasted_iota(jnp.int32, (BLOCK, BLOCK), 0)
        == lax.broadcasted_iota(jnp.int32, (BLOCK, BLOCK), 1)
    ).astype(jnp.float32)
    eliminate(work, inverse, 0, 4)
    meanwhile()
    to_x[0].wait_recv()
    half = out.at[across, level, 0]
    corner_y = sends.start(half, half, y_peer)
    to_y[1].wait_recv()
    half = out.at[along, level, 1]
    corner_x = sends.start(half, half, x_peer)
    for r in range(1, local):
        to_x[r].wait_recv()
    place = out.at[across, level]
    to_core.append(sends.start(place, place, core))
    to_y[0].wait_recv()
    place = out.at[along, level]
    to_core.append(sends.start(place, place, core))
    eliminate(work, inverse, 4, BLOCK // NB)
    corner_y.wait_recv()
    half = out.at[corner, level, 0]
    to_core.append(sends.start(half, half, core))
    corner_x.wait_recv()
    half = out.at[corner, level, 1]
    to_core.append(sends.start(half, half, core))
    mine.wait()
    for copy in to_core:
        copy.wait_recv()
    sends.finish()


ALL_FRONTS = 4
TURNS = (
    (0, 0), (0, 1), (0, 2), (1, 0), (0, 3), (2, 0), (1, 1), (1, 2),
    (3, 0), (2, 1), (2, 2), (2, 3), (1, 3), (3, 1), (3, 2), (3, 3),
)
BEFORE = (0, 1, 3, 5, 7, 8, 10, 12, 14)
BETWEEN = (4, 11, 12)
ROWS = 16
Z, ZC, XH, YH, CX, CY, CORE, META, PART, RAW = 0, 4, 8, 16, 24, 28, 32, 48, 52, 56
SCALE = 60
SHARE = 68
STEPS = 32767.0


def choose(index, values):
    out = jnp.int32(values[0])
    for i in range(1, len(values)):
        out = jnp.where(index == i, values[i], out)
    return out


def assemble_kernel(
    own, fields, parent,
    acc, shared, scales, inverse,
    codes, panels, met, counts, part_counts, tiles, parts_out, parts_in, pivot, work, column,
    send_sems, recv_sems, local_sems,
):
    level, grid, across, along = plane_peers()
    corner = (across + 2) % 4
    front = lax.axis_index("front")
    pair, inner = front + 1 - 2 * (front % 2), 3 - front
    turn = [front, pair, 2 - front // 2, 3 - 3 * (front // 2)]
    middle = (front == 1) | (front == 2)
    local, half, depth = own.shape
    levels, grids = panels.shape[2], panels.shape[1]
    spots = acc.shape[0] * acc.shape[2] // BLOCK
    width_blocks = acc.shape[2] // BLOCK
    pieces = local * local
    x_peer, y_peer, core = {"grid": across}, {"grid": along}, {"lvl": 1 - level}
    fronts = [{"front": pair}, {"front": (front + 2) % 4}, {"front": inner}]
    plane = [x_peer, y_peer, {"grid": corner}, core] + [
        {"grid": g, "lvl": 1 - level} for g in (across, along, corner)
    ]

    used = [0]
    finish = []

    def remote(src, dst, recv, device, when=None):
        copy = pltpu.make_async_remote_copy(
            src_ref=src,
            dst_ref=dst,
            send_sem=send_sems.at[used[0]],
            recv_sem=recv_sems.at[recv],
            device_id=device,
            device_id_type=pl.DeviceIdType.MESH,
        )
        used[0] += 1
        finish.append((when, copy))
        return copy

    def at(k, g, lv=level):
        return panels.at[turn[k], g, lv]

    parent_in = pltpu.make_async_copy(parent, acc, local_sems.at[0])
    own_in = pltpu.make_async_copy(own, at(0, grid), local_sems.at[1])
    for copy in [own_in, parent_in]:
        copy.start()

    met_out = [remote(codes, met.at[front], META + front, d) for d in fronts]
    z_own = remote(own, at(0, grid), Z + front, {"front": pair})
    z_own_in = remote(own, at(0, grid), Z + front, {"front": inner}, middle)
    z_on = [None] + [
        remote(at(k, grid), at(k, grid), Z + turn[k], {"front": to}, middle)
        for k, to in ((1, inner), (2, pair), (3, pair))
    ]
    by_z = jnp.logical_not(middle & (grid == 0))
    to_z = jnp.logical_not(jnp.logical_not(middle) & (grid == 0))
    zc_own = remote(at(0, corner), at(0, corner), ZC + front, {"front": pair}, by_z)
    to_x, to_y, to_core, on_x, on_y = [], [], [], {}, {}
    for k in range(4):
        mine = own if k == 0 else at(k, grid)
        to_x.append([remote(mine.at[h], at(k, grid).at[h], XH + 2 * k + h, x_peer) for h in (0, 1)])
        to_y.append([remote(mine.at[h], at(k, grid).at[h], YH + 2 * k + h, y_peer) for h in (0, 1)])
        sources = [mine, at(k, across), at(k, along), at(k, corner)]
        to_core.append([
            remote(source, at(k, g), CORE + 4 * k + p, core)
            for p, (source, g) in enumerate(zip(sources, (grid, across, along, corner)))
        ])
        x_half, y_half = at(k, across).at[0], at(k, along).at[1]
        by_y, by_x = None, None
        if k == 1:
            by_y = jnp.logical_not(middle) & (grid == 2)
            by_x = jnp.logical_not(middle) & (grid == 1)
        on_y[k] = remote(x_half, x_half, CY + k, y_peer, by_y)
        on_x[k] = remote(y_half, y_half, CX + k, x_peer, by_x)
    is_first = grid == 0
    part_out = [
        remote(parts_out.at[q], parts_in.at[front], PART + front, d, is_first)
        for q, d in zip((pair, (front + 2) % 4, inner), fronts)
    ]
    rows = pivot.at[level]
    raw_x = remote(rows, rows, RAW, x_peer, is_first)
    raw_y = remote(rows, rows, RAW, y_peer, is_first)
    raw_in = pltpu.make_async_copy(parent.at[0, :, pl.ds(0, BLOCK)], rows, local_sems.at[3])
    raw_halves = [pivot.at[level, pl.ds(h * (half // 2), half // 2)] for h in (0, 1)]
    raw_on = [
        remote(raw_halves[0], raw_halves[0], RAW + 1, y_peer, grid == 1),
        remote(raw_halves[1], raw_halves[1], RAW + 2, x_peer, grid == 2),
    ]
    scale_at = scales.at[grid, level]
    scale_out = [remote(scale_at, scale_at, SCALE + 2 * grid + level, d) for d in plane]
    pivot_core = remote(rows, rows, RAW + 3, core)

    slots = codes.shape[1]
    row, col, named, spot = [
        fields[i : i + 1, j * slots : (j + 1) * slots] for i in (0, 1) for j in (0, 1)
    ]
    blocks = fields[2:3, ALL_FRONTS : ALL_FRONTS + 1]
    live = (row * grids + grid < blocks) & (col < blocks)
    owner = jnp.zeros_like(named)
    for q in range(ALL_FRONTS):
        owner = jnp.where(named == q, fields[2:3, q : q + 1], owner)
    code = (col % grids) * (spots * pieces) + spot * pieces + row * local + col // grids
    code = jnp.where(live, code, -1)
    ids = lax.broadcasted_iota(jnp.int32, codes.shape, 0)
    codes[...] = jnp.where(owner == ids, code, -1)
    met[pl.ds(front, 1)] = codes[...][None]
    greet(fronts + plane)

    def spread(k):
        to_x[k][0].start()
        to_y[k][1].start()
        to_core[k][0].start()
        to_x[k][1].start()
        to_y[k][0].start()

    z_own.start()

    @pl.when(middle)
    def _():
        z_own_in.start()

    for copy in met_out:
        copy.start()
    spread(0)

    def pass_on(k):
        z_on_wait(k)
        z_on[k].start()

    def z_on_wait(k):
        pltpu.make_async_remote_copy(
            src_ref=at(k, grid), dst_ref=at(k, grid), send_sem=send_sems.at[0],
            recv_sem=recv_sems.at[Z + turn[k]], device_id=core, device_id_type=pl.DeviceIdType.MESH,
        ).wait_recv()

    def zc_wait(k):
        pltpu.make_async_remote_copy(
            src_ref=at(k, corner), dst_ref=at(k, corner), send_sem=send_sems.at[0],
            recv_sem=recv_sems.at[ZC + turn[k]], device_id=core, device_id_type=pl.DeviceIdType.MESH,
        ).wait_recv()

    def relay(k):
        to_x[k][0].wait_recv()
        on_y[k].start()
        to_y[k][1].wait_recv()
        on_x[k].start()

    def x_in(k):
        to_x[k][1].wait_recv()
        to_core[k][1].start()

    def y_in(k):
        to_y[k][0].wait_recv()
        to_core[k][2].start()

    def corner_in(k):
        on_x[k].wait_recv()
        on_y[k].wait_recv()
        to_core[k][3].start()

    def end_in(k):
        @pl.when(jnp.logical_not(middle))
        def _():
            z_on_wait(k)

    def sum_parts():
        for d in range(3):
            pltpu.make_async_remote_copy(
                src_ref=parts_in.at[0], dst_ref=parts_in.at[0], send_sem=send_sems.at[0],
                recv_sem=recv_sems.at[PART + (front + d + 1) % 4], device_id=core,
                device_id_type=pl.DeviceIdType.MESH,
            ).wait_recv()
        total = pivot[level] + parts_out[front]
        for d in range(3):
            total = total + parts_in[(front + d + 1) % 4]
        pivot[level] = total

    def before(i):
        if i == 0:
            own_in.wait()
            parent_in.wait()
        elif i == 1:
            relay(0)
            x_in(0)

            @pl.when(middle)
            def _():
                pass_on(1)
                pass_on(2)

            end_in(1)
            spread(1)
            y_in(0)
        elif i == 3:
            corner_in(0)
            for d in range(3):
                pltpu.make_async_remote_copy(
                    src_ref=codes, dst_ref=met.at[0], send_sem=send_sems.at[0],
                    recv_sem=recv_sems.at[META + (front + d + 1) % 4], device_id=core,
                    device_id_type=pl.DeviceIdType.MESH,
                ).wait_recv()

        elif i == 5:
            to_x[1][0].wait_recv()
            to_y[1][1].wait_recv()

            @pl.when(jnp.logical_not(middle) & (grid == 2))
            def _():
                on_y[1].start()

            @pl.when(jnp.logical_not(middle) & (grid == 1))
            def _():
                on_x[1].start()

            x_in(1)
            y_in(1)
        elif i == 7:
            relay(2)
        elif i == 8:
            end_in(3)
            spread(3)
            x_in(2)
            y_in(2)
        elif i == 10:
            corner_in(2)
        elif i == 12:

            @pl.when(is_first)
            def _():
                sum_parts()
                raw_x.start()
                raw_y.start()
        elif i == 14:
            corner_in(3)

    def between(i):
        if i == 4:

            @pl.when(middle)
            def _():
                pass_on(3)


            @pl.when(by_z)
            def _():
                zc_own.start()

            end_in(2)
            spread(2)

            @pl.when(is_first)
            def _():
                for copy in part_out:
                    copy.start()
        elif i == 11:

            @pl.when(to_z)
            def _():
                zc_wait(1)

            @pl.when(jnp.logical_not(to_z))
            def _():
                on_x[1].wait_recv()
                on_y[1].wait_recv()

            to_core[1][3].start()
        elif i == 12:
            relay(3)
            x_in(3)
            for g in (1, 2):

                @pl.when(grid == g)
                def _(g=g):
                    raw_x.wait_recv()
                    raw_on[g - 1].start()
            y_in(3)

    def expand(k, c):
        row = met[c, pl.ds(front, 1), :]
        ones = jnp.ones((row.shape[1], 128), jnp.bfloat16)
        ids = lax.broadcasted_iota(jnp.int32, (grids * spots * pieces, row.shape[1]), 0)
        hit = jnp.where(ids == row, 1.0, 0.0).astype(jnp.bfloat16)
        count = jnp.dot(hit, ones, preferred_element_type=jnp.float32)
        counts[k] = jnp.broadcast_to(
            count.reshape(grids, spots * pieces, 1, 128), (grids, spots * pieces, 8, 128)
        )

    def expand_parts():
        ids = lax.broadcasted_iota(jnp.int32, (grids * pieces, codes.shape[1]), 0)
        ids = (ids // pieces) * (spots * pieces) + ids % pieces
        ones = jnp.ones((codes.shape[1], 128), jnp.bfloat16)
        for q in range(ALL_FRONTS):
            hit = jnp.where(ids == codes[q : q + 1, :], 1.0, 0.0).astype(jnp.bfloat16)
            count = jnp.dot(hit, ones, preferred_element_type=jnp.float32)
            part_counts[q] = jnp.broadcast_to(
                count.reshape(grids * pieces, 1, 128), (grids * pieces, 8, 128)
            )

    def pick(ref, first, lane):
        value = ref[pl.ds(pl.multiple_of(first, ROWS), ROWS), lane : lane + half]
        return value.astype(jnp.float32).reshape(ROWS // 8, 8, half)

    def multiply(k, c, g):
        right = panels[c, g].reshape(levels * local * half, depth)
        left = panels[c, grid, level].reshape(local * half, depth)
        prod = lax.dot_general(left, right, NT, preferred_element_type=jnp.float32)
        tiles[...] = (-prod).astype(jnp.bfloat16)

        def add(i, carry):
            rows = pl.ds(pl.multiple_of(i * ROWS, ROWS), ROWS)
            parts = [
                [
                    pick(tiles, r * half + i * ROWS, (m * local + s) * half)
                    for r in range(local)
                    for s in range(local)
                ]
                for m in range(levels)
            ]
            for p in range(spots):
                lane = p % width_blocks * BLOCK
                many = [counts[k, g, p * pieces + x][None] for x in range(pieces)]
                for m in range(levels):
                    at = slice(lane + m * half, lane + (m + 1) * half)
                    total = acc[p // width_blocks, rows, at].reshape(ROWS // 8, 8, half)
                    for x in range(pieces):
                        total = total + many[x] * parts[m][x]
                    acc[p // width_blocks, rows, at] = total.reshape(ROWS, half)
            return carry

        lax.fori_loop(0, half // ROWS, add, 0)

    def add_parts(g):
        def add(i, carry):
            at_rows = pl.ds(pl.multiple_of(i * ROWS, ROWS), ROWS)
            for m in range(levels):
                at = slice(m * half, (m + 1) * half)
                piece = [
                    pick(tiles, r * half + i * ROWS, (m * local + s) * half)
                    for r in range(local)
                    for s in range(local)
                ]
                for q in range(ALL_FRONTS):
                    total = parts_out[q, at_rows, at].reshape(ROWS // 8, 8, half)
                    for x in range(pieces):
                        total = total + part_counts[q, g * pieces + x][None] * piece[x]
                    parts_out[q, at_rows, at] = total.reshape(ROWS, half)
            return carry

        lax.fori_loop(0, half // ROWS, add, 0)

    @pl.when(is_first)
    def _():
        raw_in.start()
        parts_out[...] = jnp.zeros_like(parts_out)
        expand_parts()
        raw_in.wait()

    def step(i, carry):
        for j in range(len(TURNS)):
            if j in BEFORE:

                @pl.when(i == j)
                def _(j=j):
                    before(j)

        k = choose(i, [t[0] for t in TURNS])
        p = choose(i, [t[1] for t in TURNS])
        c = choose(k, turn)
        g = choose(p, [grid, across, along, corner])
        pltpu.make_async_remote_copy(
            src_ref=panels.at[c, g, level], dst_ref=panels.at[c, g, level],
            send_sem=send_sems.at[0], recv_sem=recv_sems.at[CORE + 4 * k + p],
            device_id=core, device_id_type=pl.DeviceIdType.MESH,
        ).wait_recv()

        @pl.when(p == 0)
        def _():
            expand(k, c)

        multiply(k, c, g)

        @pl.when(is_first & (k == 0))
        def _():
            add_parts(g)

        for j in BETWEEN:

            @pl.when(i == j)
            def _(j=j):
                between(j)

        return carry

    lax.fori_loop(0, len(TURNS), step, 0)

    @pl.when(grid == 3)
    def _():
        raw_on[0].wait_recv()
        raw_on[1].wait_recv()

    pivot_core.start()
    peaks = []
    for r in range(local):
        value = acc[r, :, :BLOCK]
        largest = jnp.maximum(jnp.max(jnp.abs(value), axis=1, keepdims=True), 1e-30)
        value = value * (STEPS / largest)
        value = value + jnp.where(value < 0.0, -0.5, 0.5)
        column[r] = value.astype(jnp.int32).astype(jnp.int16)
        peaks.append(largest)

    def whole():
        pivot_core.wait_recv()
        return pivot[...].reshape(BLOCK, BLOCK)

    def send_scales():
        for r in range(local):
            wide = jnp.broadcast_to(peaks[r] * (1.0 / STEPS), (half, half))
            scales[grid, level, r] = wide.T[:8, :]
        for copy in scale_out:
            copy.start()

    share_body(
        column, whole, send_scales, shared, inverse, work,
        Sends(send_sems, recv_sems, used[0], SHARE), local_sems.at[4],
    )
    for g in (across, along, corner, grid):
        for lv in (level, 1 - level):
            if g is grid and lv is level:
                continue
            pltpu.make_async_remote_copy(
                src_ref=scale_at, dst_ref=scales.at[g, lv], send_sem=send_sems.at[0],
                recv_sem=recv_sems.at[SCALE + 2 * g + lv], device_id=core,
                device_id_type=pl.DeviceIdType.MESH,
            ).wait_recv()
    for when, copy in finish:
        if when is None:
            copy.wait_send()
        else:

            @pl.when(when)
            def _(copy=copy):
                copy.wait_send()


VMEM = pl.BlockSpec(memory_space=pltpu.VMEM)
HBM = pl.BlockSpec(memory_space=pltpu.HBM)
ANY = pl.BlockSpec(memory_space=pl.ANY)
SMEM = pl.BlockSpec(memory_space=pltpu.SMEM)


def owner_of(parents, parent_owner):
    ids = jnp.arange(parent_owner.shape[0], dtype=jnp.int32)
    return jnp.sum(jnp.where(parents[..., None] == ids, parent_owner, 0), axis=-1)


def assemble_all(
    child_panel, child_blocks, tile_rows, tile_cols, tile_parent, tile_place, parent_owner, parent_front
):
    levels, grids, fronts = lax.axis_size("lvl"), lax.axis_size("grid"), lax.axis_size("front")
    local, half, depth = child_panel.shape[1], child_panel.shape[4], child_panel.shape[5]
    parent_local, width = parent_front.shape[1], parent_front.shape[5]
    slots = tile_rows.shape[3]
    spots = parent_local * width // BLOCK
    pieces = local * local
    lanes = 2 * slots
    fields = [a.reshape(slots) for a in (tile_rows, tile_cols, tile_parent, tile_place)]
    fields += [parent_owner, child_blocks, jnp.zeros((lanes - fronts - 1,), jnp.int32)]
    fields = jnp.concatenate(fields).reshape(3, lanes)
    parent = parent_front.reshape(parent_local, half, width)
    sends = 110
    return pl.pallas_call(
        assemble_kernel,
        out_shape=(
            jax.ShapeDtypeStruct(parent.shape, jnp.float32),
            jax.ShapeDtypeStruct((grids, levels, parent_local, half, BLOCK), jnp.int16),
            jax.ShapeDtypeStruct((grids, levels, parent_local, 8, half), jnp.float32),
            jax.ShapeDtypeStruct((BLOCK, BLOCK), jnp.float32),
        ),
        in_specs=[ANY, VMEM, ANY],
        out_specs=(VMEM,) * 4,
        scratch_shapes=[
            pltpu.VMEM((8, slots), jnp.int32),
            pltpu.VMEM((fronts, grids, levels, local, half, depth), jnp.bfloat16),
            pltpu.VMEM((fronts, 8, slots), jnp.int32),
            pltpu.VMEM((fronts, grids, spots * pieces, 8, 128), jnp.float32),
            pltpu.VMEM((fronts, grids * pieces, 8, 128), jnp.float32),
            pltpu.VMEM((local * half, levels * local * half), jnp.bfloat16),
            pltpu.VMEM((fronts, half, BLOCK), jnp.float32),
            pltpu.VMEM((fronts, half, BLOCK), jnp.float32),
            pltpu.VMEM((levels, half, BLOCK), jnp.float32),
            pltpu.VMEM((BLOCK, 2 * BLOCK), jnp.float32),
            pltpu.VMEM((parent_local, half, BLOCK), jnp.int16),
            pltpu.SemaphoreType.DMA((sends,)),
            pltpu.SemaphoreType.DMA((SHARE + 12,)),
            pltpu.SemaphoreType.DMA((9,)),
        ],
        compiler_params=pltpu.CompilerParams(
            collective_id=0, has_side_effects=True, vmem_limit_bytes=50 * 1024 * 1024
        ),
        name="assemble",
    )(
        child_panel.reshape(local, half, depth),
        fields,
        parent,
    )


def exchange_tiles(
    child_panel, child_blocks, tile_rows, tile_cols, tile_parent, tile_place, parent_owner, parent_front
):
    levels, grids, fronts = lax.axis_size("lvl"), lax.axis_size("grid"), lax.axis_size("front")
    grid_index = lax.axis_index("grid")
    local, half, depth = child_panel.shape[1], child_panel.shape[4], child_panel.shape[5]
    parent_local, width = parent_front.shape[1], parent_front.shape[5]
    slots = tile_rows.shape[3]
    blocks = width // BLOCK
    capacity = 2 * slots // fronts
    own = child_panel.reshape(local * half, depth)
    view = lax.all_gather(
        own.reshape(1, local, half, depth), ("grid", "lvl"), axis=0, tiled=True
    ).reshape(grids, levels, local, half, depth)
    gram = jnp.einsum("ik,glsjk->isglj", own, view, preferred_element_type=jnp.float32)
    gram = (-gram).astype(jnp.bfloat16).reshape(local, half, local * grids, BLOCK)
    gram = gram.transpose(0, 2, 1, 3).reshape(local * local * grids, half, BLOCK)
    row, col = tile_rows.reshape(slots), tile_cols.reshape(slots)
    live = (row * grids + grid_index < child_blocks[0]) & (col < child_blocks[0])
    owners = owner_of(tile_parent.reshape(slots), parent_owner)
    before = (jnp.arange(slots)[:, None] > jnp.arange(slots)[None, :]).astype(jnp.int32)
    same = (owners[:, None] == owners[None, :]).astype(jnp.int32)
    rank = jnp.sum(before * same, axis=1)
    index = owners * capacity + rank
    matches = index[None, :] == jnp.arange(fronts * capacity, dtype=jnp.int32)[:, None]
    filled = jnp.any(matches & live[None, :], axis=1)
    spans = local * grids
    pick = (row * spans + col)[:, None] == jnp.arange(local * spans, dtype=jnp.int32)[None, :]
    pick = jnp.any((matches & live[None, :])[:, :, None] & pick[None], axis=1)
    place = jnp.sum(jnp.where(matches, tile_place.reshape(slots)[None, :], 0), axis=1)
    outgoing = jnp.einsum(
        "kt,tij->kij", pick.astype(jnp.bfloat16), gram, preferred_element_type=jnp.float32
    ).astype(jnp.bfloat16)
    positions = jnp.where(filled, place, -1)
    incoming = lax.all_to_all(outgoing, "front", split_axis=0, concat_axis=0, tiled=True)
    landed = lax.all_to_all(positions, "front", split_axis=0, concat_axis=0, tiled=True)
    spots = parent_local * blocks
    selector = (landed[:, None] == jnp.arange(spots, dtype=jnp.int32)[None, :]).astype(jnp.bfloat16)
    contrib = jnp.einsum("sk,sij->kij", selector, incoming, preferred_element_type=jnp.float32)
    contrib = contrib.reshape(parent_local, blocks, half, BLOCK).transpose(0, 2, 1, 3)
    assembled = parent_front.reshape(parent_local, half, width) + contrib.reshape(
        parent_local, half, width
    )
    raw = lax.all_gather(assembled[0, :, :BLOCK][None], ("grid", "lvl"), axis=0, tiled=True)
    raw = raw[:levels].reshape(levels * half, BLOCK)
    return assembled, raw


def share_columns(assembled, pivot):
    levels, grids = lax.axis_size("lvl"), lax.axis_size("grid")
    column = assembled[:, :, :BLOCK]
    return pl.pallas_call(
        share_kernel,
        out_shape=(
            jax.ShapeDtypeStruct((grids, levels) + column.shape, jnp.float32),
            jax.ShapeDtypeStruct((BLOCK, BLOCK), jnp.float32),
        ),
        in_specs=[VMEM, VMEM],
        out_specs=(VMEM, VMEM),
        scratch_shapes=[
            pltpu.VMEM((BLOCK, 2 * BLOCK), jnp.float32),
            pltpu.SemaphoreType.DMA((12,)),
            pltpu.SemaphoreType.DMA((12,)),
            pltpu.SemaphoreType.DMA,
        ],
        compiler_params=pltpu.CompilerParams(
            collective_id=1, has_side_effects=True, vmem_limit_bytes=16 * 1024 * 1024
        ),
        name="share",
    )(column, pivot)


def per_device(*args):
    parent_front = args[-1]
    if lax.axis_size("front") == ALL_FRONTS:
        assembled, *column, inverse = assemble_all(*args)
    else:
        assembled, pivot = exchange_tiles(*args)
        shared, inverse = share_columns(assembled, pivot)
        column = [shared]
    local, half, width = assembled.shape
    result = pl.pallas_call(
        schur_kernel,
        out_shape=jax.ShapeDtypeStruct(assembled.shape, jnp.float32),
        in_specs=[VMEM] * (2 + len(column)),
        out_specs=ANY,
        scratch_shapes=[
            pltpu.VMEM((width // BLOCK, local, half, BLOCK), jnp.float32),
            pltpu.SemaphoreType.DMA((width // BLOCK,)),
        ],
        compiler_params=pltpu.CompilerParams(vmem_limit_bytes=20 * 1024 * 1024),
        name="schur",
    )(assembled, inverse, *column)
    return result.reshape(parent_front.shape)


def solution(mesh):
    return jax.shard_map(
        per_device,
        mesh=mesh,
        in_specs=(
            P("front", None, "grid", "lvl", None, None),
            P("front"),
            P("lvl", "front", "grid", None),
            P("lvl", "front", "grid", None),
            P("lvl", "front", "grid", None, None),
            P("lvl", "front", "grid", None),
            P(),
            P("front", None, "grid", "lvl", None, None),
        ),
        out_specs=P("front", None, "grid", "lvl", None, None),
        check_vma=False,
    )
```

```python
import functools

import jax
import jax.numpy as jnp
from jax import lax
from jax.experimental import pallas as pl
from jax.experimental.pallas import tpu as pltpu
from jax.sharding import PartitionSpec as P

BLOCK = 256
NB = 32
SUB = 8
HIGHEST = lax.Precision.HIGHEST
HIGH = lax.Precision.HIGH
NT = (((1,), (1,)), ((), ()))
TN = (((0,), (0,)), ((), ()))


def eliminate(work, inverse, begin, end):
    n, side = BLOCK, 128
    row_ids = lax.broadcasted_iota(jnp.int32, (NB, 1), 0)
    for kb in range(begin, end):
        first = kb * NB
        base = first // side * side
        low, high = base, base + 3 * side
        tiles = (high - low) // 128
        rows = work[first : first + NB, low:high]
        for sub in range(NB // SUB):
            at = first - low + sub * SUB
            cols = [
                jnp.broadcast_to(rows[:, at + i : at + i + 1], (NB, 128)) for i in range(SUB)
            ]
            for i in range(SUB):
                j = sub * SUB + i
                head = cols[i][j : j + 1, :]
                inv, per = lax.rsqrt(head), 1.0 / head
                for m in range(i + 1, SUB):
                    cols[m] = cols[m] - (cols[i] * cols[m][j : j + 1, :]) * per
                below = jnp.where(row_ids > j, cols[i] * inv, 0.0)
                urow = rows[j : j + 1, :] * jnp.concatenate([inv] * tiles, axis=1)
                wide = jnp.concatenate([below] * tiles, axis=1)
                rows = jnp.where(row_ids == j, urow, rows - wide * urow)
        if base == 0:
            inverse[first : first + NB, :side] = rows[:, n:high]
            inverse[first : first + NB, side:] = jnp.zeros((NB, n - side), jnp.float32)
        else:
            inverse[first : first + NB, :] = rows[:, n - low :]
        if first + NB < base + side:
            update = lax.dot_general(
                rows[:, :side], rows, TN, precision=HIGHEST, preferred_element_type=jnp.float32
            )
            work[first + NB : base + side, low:high] = (
                work[first + NB : base + side, low:high] - update[first + NB - base :, :]
            )
        if base == 0:
            work[first : first + NB, low:high] = rows
        if first + NB == side:
            update = lax.dot_general(
                work[:side, side:n],
                work[:side, side : n + side],
                TN,
                precision=HIGHEST,
                preferred_element_type=jnp.float32,
            )
            work[side:, side : n + side] = work[side:, side : n + side] - update


def schur_kernel(acc, inverse, shared, *rest):
    scales = rest[0] if len(rest) == 4 else None
    out, block, sems = rest[-3:]
    local, half, width = acc.shape
    grids, levels = shared.shape[0], shared.shape[1]
    blocks = width // BLOCK

    def put(b):
        lanes = pl.ds(pl.multiple_of(b * BLOCK, BLOCK), BLOCK)
        return pltpu.make_async_copy(block.at[b], out.at[:, :, lanes], sems.at[b])

    column = acc[:, :, :BLOCK].reshape(local * half, BLOCK)
    rows = lax.dot_general(
        column, inverse[...], NT, precision=HIGHEST, preferred_element_type=jnp.float32
    )
    block[0] = rows.reshape(local, half, BLOCK)
    put(0).start()
    weights = jnp.dot(rows, inverse[...], precision=HIGHEST, preferred_element_type=jnp.float32)
    for b in range(1, blocks):
        g, s = b % grids, b // grids
        other = shared[g, :, s].reshape(levels * half, BLOCK)
        if scales is not None:
            other = other.astype(jnp.int32).astype(jnp.float32)
        prod = lax.dot_general(
            weights, other, NT, precision=HIGH, preferred_element_type=jnp.float32
        )
        if scales is not None:
            row = [scales[g, lv, s, :1, :] for lv in range(levels)]
            prod = prod * jnp.concatenate(row, axis=1)
        prod = prod.reshape(local, half, BLOCK)
        block[b] = acc[:, :, b * BLOCK : (b + 1) * BLOCK] - prod
        put(b).start()
    for b in range(blocks):
        put(b).wait()


class Sends:
    def __init__(self, send_sems, recv_sems, first_send=0, first_recv=0):
        self.send_sems, self.recv_sems, self.started = send_sems, recv_sems, []
        self.first_send, self.first_recv, self.used = first_send, first_recv, 0

    def make(self, src, dst, device):
        copy = pltpu.make_async_remote_copy(
            src_ref=src,
            dst_ref=dst,
            send_sem=self.send_sems.at[self.first_send + self.used],
            recv_sem=self.recv_sems.at[self.first_recv + self.used],
            device_id=device,
            device_id_type=pl.DeviceIdType.MESH,
        )
        self.used += 1
        return copy

    def start(self, src, dst, device):
        copy = self.make(src, dst, device)
        copy.start()
        self.started.append(copy)
        return copy

    def finish(self):
        for copy in self.started:
            copy.wait_send()


def greet(devices):
    barrier = pltpu.get_barrier_semaphore()
    for device in devices:
        pl.semaphore_signal(barrier, inc=1, device_id=device, device_id_type=pl.DeviceIdType.MESH)
    pl.semaphore_wait(barrier, len(devices))


def plane_peers():
    level, grid = lax.axis_index("lvl"), lax.axis_index("grid")
    across = grid + 1 - 2 * (grid % 2)
    along = (grid + 2) % 4
    return level, grid, across, along


def share_kernel(own, pivot, out, inverse, work, send_sems, recv_sems, local_sem):
    level, grid, across, along = plane_peers()
    greet([{"grid": across}, {"grid": along}, {"lvl": 1 - level}])
    share_body(own, lambda: pivot[...], lambda: None, out, inverse, work, Sends(send_sems, recv_sems), local_sem)


def share_body(own, whole_pivot, meanwhile, out, inverse, work, sends, local_sem):
    level, grid, across, along = plane_peers()
    corner = (across + 2) % 4
    x_peer, y_peer, core = {"grid": across}, {"grid": along}, {"lvl": 1 - level}
    local = out.shape[2]
    mine = pltpu.make_async_copy(own, out.at[grid, level], local_sem)
    to_x = [None] * local
    to_y = [None] * local
    to_core = []
    for r in range(local):
        place = out.at[grid, level, r]
        to_x[r] = sends.start(own.at[r], place, x_peer)
        place = out.at[grid, level, local - 1 - r]
        to_y[local - 1 - r] = sends.start(own.at[local - 1 - r], place, y_peer)
    to_core.append(sends.start(own, out.at[grid, level], core))
    mine.start()
    whole = whole_pivot()
    work[:, :BLOCK] = 0.5 * (whole + whole.T)
    work[:, BLOCK:] = (
        lax.broadcasted_iota(jnp.int32, (BLOCK, BLOCK), 0)
        == lax.broadcasted_iota(jnp.int32, (BLOCK, BLOCK), 1)
    ).astype(jnp.float32)
    eliminate(work, inverse, 0, 4)
    meanwhile()
    to_x[0].wait_recv()
    half = out.at[across, level, 0]
    corner_y = sends.start(half, half, y_peer)
    to_y[1].wait_recv()
    half = out.at[along, level, 1]
    corner_x = sends.start(half, half, x_peer)
    for r in range(1, local):
        to_x[r].wait_recv()
    place = out.at[across, level]
    to_core.append(sends.start(place, place, core))
    to_y[0].wait_recv()
    place = out.at[along, level]
    to_core.append(sends.start(place, place, core))
    eliminate(work, inverse, 4, BLOCK // NB)
    corner_y.wait_recv()
    half = out.at[corner, level, 0]
    to_core.append(sends.start(half, half, core))
    corner_x.wait_recv()
    half = out.at[corner, level, 1]
    to_core.append(sends.start(half, half, core))
    mine.wait()
    for copy in to_core:
        copy.wait_recv()
    sends.finish()


ALL_FRONTS = 4
TURNS = (
    (0, 0), (0, 1), (0, 2), (1, 0), (0, 3), (2, 0), (1, 1), (1, 2),
    (3, 0), (2, 1), (2, 2), (2, 3), (1, 3), (3, 1), (3, 2), (3, 3),
)
BEFORE = (0, 1, 3, 5, 7, 8, 10, 12, 14)
BETWEEN = (4, 11, 12)
ROWS = 16
Z, ZC, XH, YH, CX, CY, CORE, META, PART, RAW = 0, 4, 8, 16, 24, 28, 32, 48, 52, 56
SCALE = 60
SHARE = 68
STEPS = 32767.0


def choose(index, values):
    out = jnp.int32(values[0])
    for i in range(1, len(values)):
        out = jnp.where(index == i, values[i], out)
    return out


def assemble_kernel(
    own, fields, parent,
    acc, shared, scales, inverse,
    codes, panels, met, counts, part_counts, tiles, parts_out, parts_in, pivot, work, column,
    send_sems, recv_sems, local_sems,
):
    level, grid, across, along = plane_peers()
    corner = (across + 2) % 4
    front = lax.axis_index("front")
    pair, inner = front + 1 - 2 * (front % 2), 3 - front
    turn = [front, pair, 2 - front // 2, 3 - 3 * (front // 2)]
    middle = (front == 1) | (front == 2)
    local, half, depth = own.shape
    levels, grids = panels.shape[2], panels.shape[1]
    spots = acc.shape[0] * acc.shape[2] // BLOCK
    width_blocks = acc.shape[2] // BLOCK
    pieces = local * local
    x_peer, y_peer, core = {"grid": across}, {"grid": along}, {"lvl": 1 - level}
    fronts = [{"front": pair}, {"front": (front + 2) % 4}, {"front": inner}]
    plane = [x_peer, y_peer, {"grid": corner}, core] + [
        {"grid": g, "lvl": 1 - level} for g in (across, along, corner)
    ]

    used = [0]
    finish = []

    def remote(src, dst, recv, device, when=None):
        copy = pltpu.make_async_remote_copy(
            src_ref=src,
            dst_ref=dst,
            send_sem=send_sems.at[used[0]],
            recv_sem=recv_sems.at[recv],
            device_id=device,
            device_id_type=pl.DeviceIdType.MESH,
        )
        used[0] += 1
        finish.append((when, copy))
        return copy

    def at(k, g, lv=level):
        return panels.at[turn[k], g, lv]

    parent_in = pltpu.make_async_copy(parent, acc, local_sems.at[0])
    own_in = pltpu.make_async_copy(own, at(0, grid), local_sems.at[1])
    for copy in [own_in, parent_in]:
        copy.start()

    met_out = [remote(codes, met.at[front], META + front, d) for d in fronts]
    z_own = remote(own, at(0, grid), Z + front, {"front": pair})
    z_own_in = remote(own, at(0, grid), Z + front, {"front": inner}, middle)
    z_on = [None] + [
        remote(at(k, grid), at(k, grid), Z + turn[k], {"front": to}, middle)
        for k, to in ((1, inner), (2, pair), (3, pair))
    ]
    by_z = jnp.logical_not(middle & (grid == 0))
    to_z = jnp.logical_not(jnp.logical_not(middle) & (grid == 0))
    zc_own = remote(at(0, corner), at(0, corner), ZC + front, {"front": pair}, by_z)
    to_x, to_y, to_core, on_x, on_y = [], [], [], {}, {}
    for k in range(4):
        mine = own if k == 0 else at(k, grid)
        to_x.append([remote(mine.at[h], at(k, grid).at[h], XH + 2 * k + h, x_peer) for h in (0, 1)])
        to_y.append([remote(mine.at[h], at(k, grid).at[h], YH + 2 * k + h, y_peer) for h in (0, 1)])
        sources = [mine, at(k, across), at(k, along), at(k, corner)]
        to_core.append([
            remote(source, at(k, g), CORE + 4 * k + p, core)
            for p, (source, g) in enumerate(zip(sources, (grid, across, along, corner)))
        ])
        x_half, y_half = at(k, across).at[0], at(k, along).at[1]
        by_y, by_x = None, None
        if k == 1:
            by_y = jnp.logical_not(middle) & (grid == 2)
            by_x = jnp.logical_not(middle) & (grid == 1)
        on_y[k] = remote(x_half, x_half, CY + k, y_peer, by_y)
        on_x[k] = remote(y_half, y_half, CX + k, x_peer, by_x)
    is_first = grid == 0
    part_out = [
        remote(parts_out.at[q], parts_in.at[front], PART + front, d, is_first)
        for q, d in zip((pair, (front + 2) % 4, inner), fronts)
    ]
    rows = pivot.at[level]
    raw_x = remote(rows, rows, RAW, x_peer, is_first)
    raw_y = remote(rows, rows, RAW, y_peer, is_first)
    raw_in = pltpu.make_async_copy(parent.at[0, :, pl.ds(0, BLOCK)], rows, local_sems.at[3])
    raw_halves = [pivot.at[level, pl.ds(h * (half // 2), half // 2)] for h in (0, 1)]
    raw_on = [
        remote(raw_halves[0], raw_halves[0], RAW + 1, y_peer, grid == 1),
        remote(raw_halves[1], raw_halves[1], RAW + 2, x_peer, grid == 2),
    ]
    scale_at = scales.at[grid, level]
    scale_out = [remote(scale_at, scale_at, SCALE + 2 * grid + level, d) for d in plane]
    pivot_core = remote(rows, rows, RAW + 3, core)

    greet(fronts + plane)

    def spread(k):
        to_x[k][0].start()
        to_y[k][1].start()
        to_core[k][0].start()
        to_x[k][1].start()
        to_y[k][0].start()

    z_own.start()

    @pl.when(middle)
    def _():
        z_own_in.start()

    spread(0)
    slots = codes.shape[1]
    row, col, named, spot = [
        fields[i : i + 1, j * slots : (j + 1) * slots] for i in (0, 1) for j in (0, 1)
    ]
    blocks = fields[2:3, ALL_FRONTS : ALL_FRONTS + 1]
    live = (row * grids + grid < blocks) & (col < blocks)
    owner = jnp.zeros_like(named)
    for q in range(ALL_FRONTS):
        owner = jnp.where(named == q, fields[2:3, q : q + 1], owner)
    code = (col % grids) * (spots * pieces) + spot * pieces + row * local + col // grids
    code = jnp.where(live, code, -1)
    ids = lax.broadcasted_iota(jnp.int32, codes.shape, 0)
    codes[...] = jnp.where(owner == ids, code, -1)
    met[pl.ds(front, 1)] = codes[...][None]
    for copy in met_out:
        copy.start()

    def pass_on(k):
        z_on_wait(k)
        z_on[k].start()

    def z_on_wait(k):
        pltpu.make_async_remote_copy(
            src_ref=at(k, grid), dst_ref=at(k, grid), send_sem=send_sems.at[0],
            recv_sem=recv_sems.at[Z + turn[k]], device_id=core, device_id_type=pl.DeviceIdType.MESH,
        ).wait_recv()

    def zc_wait(k):
        pltpu.make_async_remote_copy(
            src_ref=at(k, corner), dst_ref=at(k, corner), send_sem=send_sems.at[0],
            recv_sem=recv_sems.at[ZC + turn[k]], device_id=core, device_id_type=pl.DeviceIdType.MESH,
        ).wait_recv()

    def relay(k):
        to_x[k][0].wait_recv()
        on_y[k].start()
        to_y[k][1].wait_recv()
        on_x[k].start()

    def x_in(k):
        to_x[k][1].wait_recv()
        to_core[k][1].start()

    def y_in(k):
        to_y[k][0].wait_recv()
        to_core[k][2].start()

    def corner_in(k):
        on_x[k].wait_recv()
        on_y[k].wait_recv()
        to_core[k][3].start()

    def end_in(k):
        @pl.when(jnp.logical_not(middle))
        def _():
            z_on_wait(k)

    def sum_parts():
        for d in range(3):
            pltpu.make_async_remote_copy(
                src_ref=parts_in.at[0], dst_ref=parts_in.at[0], send_sem=send_sems.at[0],
                recv_sem=recv_sems.at[PART + (front + d + 1) % 4], device_id=core,
                device_id_type=pl.DeviceIdType.MESH,
            ).wait_recv()
        total = pivot[level] + parts_out[front]
        for d in range(3):
            total = total + parts_in[(front + d + 1) % 4]
        pivot[level] = total

    def before(i):
        if i == 0:
            own_in.wait()
            parent_in.wait()
        elif i == 1:
            relay(0)
            x_in(0)

            @pl.when(middle)
            def _():
                pass_on(1)
                pass_on(2)

            end_in(1)
            spread(1)
            y_in(0)
        elif i == 3:
            corner_in(0)
            for d in range(3):
                pltpu.make_async_remote_copy(
                    src_ref=codes, dst_ref=met.at[0], send_sem=send_sems.at[0],
                    recv_sem=recv_sems.at[META + (front + d + 1) % 4], device_id=core,
                    device_id_type=pl.DeviceIdType.MESH,
                ).wait_recv()

        elif i == 5:
            to_x[1][0].wait_recv()
            to_y[1][1].wait_recv()

            @pl.when(jnp.logical_not(middle) & (grid == 2))
            def _():
                on_y[1].start()

            @pl.when(jnp.logical_not(middle) & (grid == 1))
            def _():
                on_x[1].start()

            x_in(1)
            y_in(1)
        elif i == 7:
            relay(2)
        elif i == 8:
            end_in(3)
            spread(3)
            x_in(2)
            y_in(2)
        elif i == 10:
            corner_in(2)
        elif i == 12:

            @pl.when(is_first)
            def _():
                sum_parts()
                raw_x.start()
                raw_y.start()
        elif i == 14:
            corner_in(3)

    def between(i):
        if i == 4:

            @pl.when(middle)
            def _():
                pass_on(3)


            @pl.when(by_z)
            def _():
                zc_own.start()

            end_in(2)
            spread(2)

            @pl.when(is_first)
            def _():
                for copy in part_out:
                    copy.start()
        elif i == 11:

            @pl.when(to_z)
            def _():
                zc_wait(1)

            @pl.when(jnp.logical_not(to_z))
            def _():
                on_x[1].wait_recv()
                on_y[1].wait_recv()

            to_core[1][3].start()
        elif i == 12:
            relay(3)
            x_in(3)
            for g in (1, 2):

                @pl.when(grid == g)
                def _(g=g):
                    raw_x.wait_recv()
                    raw_on[g - 1].start()
            y_in(3)

    def expand(k, c):
        row = met[c, pl.ds(front, 1), :]
        ones = jnp.ones((row.shape[1], 128), jnp.bfloat16)
        ids = lax.broadcasted_iota(jnp.int32, (grids * spots * pieces, row.shape[1]), 0)
        hit = jnp.where(ids == row, 1.0, 0.0).astype(jnp.bfloat16)
        count = jnp.dot(hit, ones, preferred_element_type=jnp.float32)
        counts[k] = jnp.broadcast_to(
            count.reshape(grids, spots * pieces, 1, 128), (grids, spots * pieces, 8, 128)
        )

    def expand_parts():
        ids = lax.broadcasted_iota(jnp.int32, (grids * pieces, codes.shape[1]), 0)
        ids = (ids // pieces) * (spots * pieces) + ids % pieces
        ones = jnp.ones((codes.shape[1], 128), jnp.bfloat16)
        for q in range(ALL_FRONTS):
            hit = jnp.where(ids == codes[q : q + 1, :], 1.0, 0.0).astype(jnp.bfloat16)
            count = jnp.dot(hit, ones, preferred_element_type=jnp.float32)
            part_counts[q] = jnp.broadcast_to(
                count.reshape(grids * pieces, 1, 128), (grids * pieces, 8, 128)
            )

    def pick(ref, first, lane):
        value = ref[pl.ds(pl.multiple_of(first, ROWS), ROWS), lane : lane + half]
        return value.astype(jnp.float32).reshape(ROWS // 8, 8, half)

    def multiply(k, c, g):
        right = panels[c, g].reshape(levels * local * half, depth)
        left = panels[c, grid, level].reshape(local * half, depth)
        prod = lax.dot_general(left, right, NT, preferred_element_type=jnp.float32)
        tiles[...] = (-prod).astype(jnp.bfloat16)

        def add(i, carry):
            rows = pl.ds(pl.multiple_of(i * ROWS, ROWS), ROWS)
            parts = [
                [
                    pick(tiles, r * half + i * ROWS, (m * local + s) * half)
                    for r in range(local)
                    for s in range(local)
                ]
                for m in range(levels)
            ]
            for p in range(spots):
                lane = p % width_blocks * BLOCK
                many = [counts[k, g, p * pieces + x][None] for x in range(pieces)]
                for m in range(levels):
                    at = slice(lane + m * half, lane + (m + 1) * half)
                    total = acc[p // width_blocks, rows, at].reshape(ROWS // 8, 8, half)
                    for x in range(pieces):
                        total = total + many[x] * parts[m][x]
                    acc[p // width_blocks, rows, at] = total.reshape(ROWS, half)
            return carry

        lax.fori_loop(0, half // ROWS, add, 0)

    def add_parts(g):
        def add(i, carry):
            at_rows = pl.ds(pl.multiple_of(i * ROWS, ROWS), ROWS)
            for m in range(levels):
                at = slice(m * half, (m + 1) * half)
                piece = [
                    pick(tiles, r * half + i * ROWS, (m * local + s) * half)
                    for r in range(local)
                    for s in range(local)
                ]
                for q in range(ALL_FRONTS):
                    total = parts_out[q, at_rows, at].reshape(ROWS // 8, 8, half)
                    for x in range(pieces):
                        total = total + part_counts[q, g * pieces + x][None] * piece[x]
                    parts_out[q, at_rows, at] = total.reshape(ROWS, half)
            return carry

        lax.fori_loop(0, half // ROWS, add, 0)

    @pl.when(is_first)
    def _():
        raw_in.start()
        parts_out[...] = jnp.zeros_like(parts_out)
        expand_parts()
        raw_in.wait()

    def step(i, carry):
        for j in range(len(TURNS)):
            if j in BEFORE:

                @pl.when(i == j)
                def _(j=j):
                    before(j)

        k = choose(i, [t[0] for t in TURNS])
        p = choose(i, [t[1] for t in TURNS])
        c = choose(k, turn)
        g = choose(p, [grid, across, along, corner])
        pltpu.make_async_remote_copy(
            src_ref=panels.at[c, g, level], dst_ref=panels.at[c, g, level],
            send_sem=send_sems.at[0], recv_sem=recv_sems.at[CORE + 4 * k + p],
            device_id=core, device_id_type=pl.DeviceIdType.MESH,
        ).wait_recv()

        @pl.when(p == 0)
        def _():
            expand(k, c)

        multiply(k, c, g)

        @pl.when(is_first & (k == 0))
        def _():
            add_parts(g)

        for j in BETWEEN:

            @pl.when(i == j)
            def _(j=j):
                between(j)

        return carry

    lax.fori_loop(0, len(TURNS), step, 0)

    @pl.when(grid == 3)
    def _():
        raw_on[0].wait_recv()
        raw_on[1].wait_recv()

    pivot_core.start()
    peaks = []
    for r in range(local):
        value = acc[r, :, :BLOCK]
        largest = jnp.maximum(jnp.max(jnp.abs(value), axis=1, keepdims=True), 1e-30)
        value = value * (STEPS / largest)
        value = value + jnp.where(value < 0.0, -0.5, 0.5)
        column[r] = value.astype(jnp.int32).astype(jnp.int16)
        peaks.append(largest)

    def whole():
        pivot_core.wait_recv()
        return pivot[...].reshape(BLOCK, BLOCK)

    def send_scales():
        for r in range(local):
            wide = jnp.broadcast_to(peaks[r] * (1.0 / STEPS), (half, half))
            scales[grid, level, r] = wide.T[:8, :]
        for copy in scale_out:
            copy.start()

    share_body(
        column, whole, send_scales, shared, inverse, work,
        Sends(send_sems, recv_sems, used[0], SHARE), local_sems.at[4],
    )
    for g in (across, along, corner, grid):
        for lv in (level, 1 - level):
            if g is grid and lv is level:
                continue
            pltpu.make_async_remote_copy(
                src_ref=scale_at, dst_ref=scales.at[g, lv], send_sem=send_sems.at[0],
                recv_sem=recv_sems.at[SCALE + 2 * g + lv], device_id=core,
                device_id_type=pl.DeviceIdType.MESH,
            ).wait_recv()
    for when, copy in finish:
        if when is None:
            copy.wait_send()
        else:

            @pl.when(when)
            def _(copy=copy):
                copy.wait_send()


VMEM = pl.BlockSpec(memory_space=pltpu.VMEM)
HBM = pl.BlockSpec(memory_space=pltpu.HBM)
ANY = pl.BlockSpec(memory_space=pl.ANY)
SMEM = pl.BlockSpec(memory_space=pltpu.SMEM)


def owner_of(parents, parent_owner):
    ids = jnp.arange(parent_owner.shape[0], dtype=jnp.int32)
    return jnp.sum(jnp.where(parents[..., None] == ids, parent_owner, 0), axis=-1)


def assemble_all(
    child_panel, child_blocks, tile_rows, tile_cols, tile_parent, tile_place, parent_owner, parent_front
):
    levels, grids, fronts = lax.axis_size("lvl"), lax.axis_size("grid"), lax.axis_size("front")
    local, half, depth = child_panel.shape[1], child_panel.shape[4], child_panel.shape[5]
    parent_local, width = parent_front.shape[1], parent_front.shape[5]
    slots = tile_rows.shape[3]
    spots = parent_local * width // BLOCK
    pieces = local * local
    lanes = 2 * slots
    fields = [a.reshape(slots) for a in (tile_rows, tile_cols, tile_parent, tile_place)]
    fields += [parent_owner, child_blocks, jnp.zeros((lanes - fronts - 1,), jnp.int32)]
    fields = jnp.concatenate(fields).reshape(3, lanes)
    parent = parent_front.reshape(parent_local, half, width)
    sends = 110
    return pl.pallas_call(
        assemble_kernel,
        out_shape=(
            jax.ShapeDtypeStruct(parent.shape, jnp.float32),
            jax.ShapeDtypeStruct((grids, levels, parent_local, half, BLOCK), jnp.int16),
            jax.ShapeDtypeStruct((grids, levels, parent_local, 8, half), jnp.float32),
            jax.ShapeDtypeStruct((BLOCK, BLOCK), jnp.float32),
        ),
        in_specs=[ANY, VMEM, ANY],
        out_specs=(VMEM,) * 4,
        scratch_shapes=[
            pltpu.VMEM((8, slots), jnp.int32),
            pltpu.VMEM((fronts, grids, levels, local, half, depth), jnp.bfloat16),
            pltpu.VMEM((fronts, 8, slots), jnp.int32),
            pltpu.VMEM((fronts, grids, spots * pieces, 8, 128), jnp.float32),
            pltpu.VMEM((fronts, grids * pieces, 8, 128), jnp.float32),
            pltpu.VMEM((local * half, levels * local * half), jnp.bfloat16),
            pltpu.VMEM((fronts, half, BLOCK), jnp.float32),
            pltpu.VMEM((fronts, half, BLOCK), jnp.float32),
            pltpu.VMEM((levels, half, BLOCK), jnp.float32),
            pltpu.VMEM((BLOCK, 2 * BLOCK), jnp.float32),
            pltpu.VMEM((parent_local, half, BLOCK), jnp.int16),
            pltpu.SemaphoreType.DMA((sends,)),
            pltpu.SemaphoreType.DMA((SHARE + 12,)),
            pltpu.SemaphoreType.DMA((9,)),
        ],
        compiler_params=pltpu.CompilerParams(
            collective_id=0, has_side_effects=True, vmem_limit_bytes=50 * 1024 * 1024
        ),
        name="assemble",
    )(
        child_panel.reshape(local, half, depth),
        fields,
        parent,
    )


def exchange_tiles(
    child_panel, child_blocks, tile_rows, tile_cols, tile_parent, tile_place, parent_owner, parent_front
):
    levels, grids, fronts = lax.axis_size("lvl"), lax.axis_size("grid"), lax.axis_size("front")
    grid_index = lax.axis_index("grid")
    local, half, depth = child_panel.shape[1], child_panel.shape[4], child_panel.shape[5]
    parent_local, width = parent_front.shape[1], parent_front.shape[5]
    slots = tile_rows.shape[3]
    blocks = width // BLOCK
    capacity = 2 * slots // fronts
    own = child_panel.reshape(local * half, depth)
    view = lax.all_gather(
        own.reshape(1, local, half, depth), ("grid", "lvl"), axis=0, tiled=True
    ).reshape(grids, levels, local, half, depth)
    gram = jnp.einsum("ik,glsjk->isglj", own, view, preferred_element_type=jnp.float32)
    gram = (-gram).astype(jnp.bfloat16).reshape(local, half, local * grids, BLOCK)
    gram = gram.transpose(0, 2, 1, 3).reshape(local * local * grids, half, BLOCK)
    row, col = tile_rows.reshape(slots), tile_cols.reshape(slots)
    live = (row * grids + grid_index < child_blocks[0]) & (col < child_blocks[0])
    owners = owner_of(tile_parent.reshape(slots), parent_owner)
    before = (jnp.arange(slots)[:, None] > jnp.arange(slots)[None, :]).astype(jnp.int32)
    same = (owners[:, None] == owners[None, :]).astype(jnp.int32)
    rank = jnp.sum(before * same, axis=1)
    index = owners * capacity + rank
    matches = index[None, :] == jnp.arange(fronts * capacity, dtype=jnp.int32)[:, None]
    filled = jnp.any(matches & live[None, :], axis=1)
    spans = local * grids
    pick = (row * spans + col)[:, None] == jnp.arange(local * spans, dtype=jnp.int32)[None, :]
    pick = jnp.any((matches & live[None, :])[:, :, None] & pick[None], axis=1)
    place = jnp.sum(jnp.where(matches, tile_place.reshape(slots)[None, :], 0), axis=1)
    outgoing = jnp.einsum(
        "kt,tij->kij", pick.astype(jnp.bfloat16), gram, preferred_element_type=jnp.float32
    ).astype(jnp.bfloat16)
    positions = jnp.where(filled, place, -1)
    incoming = lax.all_to_all(outgoing, "front", split_axis=0, concat_axis=0, tiled=True)
    landed = lax.all_to_all(positions, "front", split_axis=0, concat_axis=0, tiled=True)
    spots = parent_local * blocks
    selector = (landed[:, None] == jnp.arange(spots, dtype=jnp.int32)[None, :]).astype(jnp.bfloat16)
    contrib = jnp.einsum("sk,sij->kij", selector, incoming, preferred_element_type=jnp.float32)
    contrib = contrib.reshape(parent_local, blocks, half, BLOCK).transpose(0, 2, 1, 3)
    assembled = parent_front.reshape(parent_local, half, width) + contrib.reshape(
        parent_local, half, width
    )
    raw = lax.all_gather(assembled[0, :, :BLOCK][None], ("grid", "lvl"), axis=0, tiled=True)
    raw = raw[:levels].reshape(levels * half, BLOCK)
    return assembled, raw


def share_columns(assembled, pivot):
    levels, grids = lax.axis_size("lvl"), lax.axis_size("grid")
    column = assembled[:, :, :BLOCK]
    return pl.pallas_call(
        share_kernel,
        out_shape=(
            jax.ShapeDtypeStruct((grids, levels) + column.shape, jnp.float32),
            jax.ShapeDtypeStruct((BLOCK, BLOCK), jnp.float32),
        ),
        in_specs=[VMEM, VMEM],
        out_specs=(VMEM, VMEM),
        scratch_shapes=[
            pltpu.VMEM((BLOCK, 2 * BLOCK), jnp.float32),
            pltpu.SemaphoreType.DMA((12,)),
            pltpu.SemaphoreType.DMA((12,)),
            pltpu.SemaphoreType.DMA,
        ],
        compiler_params=pltpu.CompilerParams(
            collective_id=1, has_side_effects=True, vmem_limit_bytes=16 * 1024 * 1024
        ),
        name="share",
    )(column, pivot)


def per_device(*args):
    parent_front = args[-1]
    if lax.axis_size("front") == ALL_FRONTS:
        assembled, *column, inverse = assemble_all(*args)
    else:
        assembled, pivot = exchange_tiles(*args)
        shared, inverse = share_columns(assembled, pivot)
        column = [shared]
    local, half, width = assembled.shape
    result = pl.pallas_call(
        schur_kernel,
        out_shape=jax.ShapeDtypeStruct(assembled.shape, jnp.float32),
        in_specs=[VMEM] * (2 + len(column)),
        out_specs=ANY,
        scratch_shapes=[
            pltpu.VMEM((width // BLOCK, local, half, BLOCK), jnp.float32),
            pltpu.SemaphoreType.DMA((width // BLOCK,)),
        ],
        compiler_params=pltpu.CompilerParams(vmem_limit_bytes=20 * 1024 * 1024),
        name="schur",
    )(assembled, inverse, *column)
    return result.reshape(parent_front.shape)


def solution(mesh):
    return jax.shard_map(
        per_device,
        mesh=mesh,
        in_specs=(
            P("front", None, "grid", "lvl", None, None),
            P("front"),
            P("lvl", "front", "grid", None),
            P("lvl", "front", "grid", None),
            P("lvl", "front", "grid", None, None),
            P("lvl", "front", "grid", None),
            P(),
            P("front", None, "grid", "lvl", None, None),
        ),
        out_specs=P("front", None, "grid", "lvl", None, None),
        check_vma=False,
    )
```
